32 devices in a mesh: ctx: 8 (over z, y), head: 4 (over x, core).
Axes of the slice: x: 2, y: 2, z: 4, core: 2. Of those that a mesh axis runs over, the one named last changes fastest.
Arguments:
- queries: bfloat16 [8192, 4096], P('ctx', 'head'), may hold values from -180 to 180
- key_rows: bfloat16 [8192, 4096], P('ctx', 'head'), may hold values from -7 to 7
- value_rows: bfloat16 [8192, 4096], P('ctx', 'head'), may hold values from -6 to 6
- out_grad: bfloat16 [8192, 4096], P('ctx', 'head'), may hold values from -6 to 6
- norm_gain: float32 [4096], P('head'), may hold values from 0.5 to 1.5
- offsets: int32 [3, 32], P(None, 'head'), may hold values from 0 to 7
- segments: int32 [8192], replicated, may hold values from 0 to 7, never falling along the last dimension, each value on 1 to 2048 neighbouring positions
- tile_mask: int32 [64, 3], P('ctx'), may hold values 0 or 1
Outputs:
- normed: bfloat16 [8192, 4096], P('ctx', 'head')
- grad_queries: bfloat16 [8192, 4096], P('ctx', 'head')
- grad_keys: bfloat16 [8192, 4096], P('ctx', 'head')
- grad_values: bfloat16 [8192, 4096], P('ctx', 'head')
The draws below stay inside these ranges and needn't reach their ends.
All inputs are finite; a program needn't handle non-finite values. No bound on the sum of `tile_mask` on one device may be relied on, other than what follows from the above.
Results may differ from the reference program's by a relative error of at most 0.006.
Values may be sent and summed in bfloat16 or wider, within the bound.
No kernel may reach another device: no remote copies, remote signals or barrier semaphores. Data moves between devices by JAX's collectives and lax.ppermute only.
A program may use at most 256 MiB of HBM per device.

```python
import math
import jax
import jax.numpy as jnp
import numpy as np
from jax import lax

D = 4096
H = 32
DH = 128
TOK_DEV = 1024
RATE = 8
LEVELS = 3
TILE = 128
SEGS = 8
TOKENS = 8192
SAMPLED = 128
TILES = 64
N_CTX = 8


def drawn_pair(key):
    base_q = jnp.clip(jax.random.normal(jax.random.fold_in(key, 101), (TOKENS, D), jnp.float32), -6.0, 6.0)
    base_k = jnp.clip(jax.random.normal(jax.random.fold_in(key, 202), (TOKENS, D), jnp.float32), -6.0, 6.0)
    return (base_q, base_k)


def draw_queries(key, part):
    return drawn_pair(key)[0].astype(jnp.bfloat16)


def draw_key_rows(key, part):
    return drawn_pair(key)[1].astype(jnp.bfloat16)


def with_ends(values, stream_key, low, high):
    longest = values.shape.index(max(values.shape))
    spots = []
    for shift in (0, 1):
        where = [jax.random.randint(jax.random.fold_in(stream_key, axis), (), 0, length) for axis, length in enumerate(values.shape)]
        where[longest] = (where[longest] + shift) % values.shape[longest]
        spots.append(tuple(where))
    return values.at[spots[0]].set(low).at[spots[1]].set(high)


def levels(key, shape, shards, smallest, largest):
    level = 1.0
    for position, shards_of in shards:
        draws = jax.random.uniform(jax.random.fold_in(jax.random.fold_in(key, 6), position), (shards_of,), jnp.float32, smallest / len(shards), largest / len(shards))
        level = level * jnp.repeat(jnp.exp(draws), shape[position] // shards_of).reshape((-1,) + (1,) * (len(shape) - 1 - position))
    return level


def profile(amount, total, most, slope):
    loads = [(1 << 20) // math.isqrt(standing ** slope) + 1 for standing in range(2, amount + 1)]
    spare, counts = total - most - (amount - 1), [1] * (amount - 1)
    while spare > 0:
        movable = [i for i in range(amount - 1) if counts[i] < most]
        whole, remaining = sum([loads[i] for i in movable]), spare
        for i in movable:
            addition = min(most - counts[i], max(1, remaining * loads[i] // whole), spare)
            counts[i] = counts[i] + addition
            spare = spare - addition
    return np.array([most] + counts)


def ragged_sizes(stream_key, number_of, total, reach, slope):
    if number_of == 2:
        one = jax.random.randint(stream_key, (), max(1, total - reach), min(reach, total - 1) + 1)
        return jnp.stack([one, total - one])
    sizes = jnp.asarray(profile(number_of, total, reach, slope), jnp.int32)
    pairs = (number_of - 1) // 2
    giver, sink = sizes[1:1 + 2 * pairs:2], sizes[2:2 + 2 * pairs:2]
    room = jnp.minimum(giver - 1, reach - sink)
    shifted = jax.random.randint(jax.random.fold_in(stream_key, 1), (pairs,), 0, 1 << 20) % (room + 1)
    sizes = sizes.at[1:1 + 2 * pairs:2].set(giver - shifted).at[2:2 + 2 * pairs:2].set(sink + shifted)
    return sizes[jax.random.permutation(jax.random.fold_in(stream_key, 2), number_of)]


def normal_values(own_key, shape, spread, reach, pieces=(), kind=jnp.bfloat16):
    values = spread * jax.random.normal(own_key, shape, jnp.float32)
    if pieces:
        values = values * levels(own_key, shape, pieces, -0.22, 0.18)
    return jnp.clip(values, -reach, reach).astype(kind)


def setup_inputs(seed: int = 0) -> dict:
    seeds = jax.random.split(jax.random.key(seed), 9)
    return {
        "queries": draw_queries(jax.random.fold_in(seeds[8], 71), 0),
        "key_rows": draw_key_rows(jax.random.fold_in(seeds[8], 71), 0),
        "value_rows": normal_values(seeds[2], (TOKENS, D), 1.0, 6.0, ((0, 8), (1, 4))),
        "out_grad": normal_values(seeds[3], (TOKENS, D), 1.0, 6.0, ((0, 8), (1, 4))),
        "norm_gain": jnp.clip(1.0 + 0.1 * jax.random.normal(seeds[4], (D,), jnp.float32), 0.5, 1.5),
        "offsets": with_ends(jax.random.randint(seeds[5], (LEVELS, H), 0, RATE), jax.random.fold_in(seeds[5], 1), 0, RATE - 1).astype(jnp.int32),
        "segments": jnp.searchsorted(jnp.cumsum(ragged_sizes(seeds[6], SEGS, TOKENS, TOKENS // 4, 0)), jnp.arange(TOKENS), side="right").astype(jnp.int32),
        "tile_mask": with_ends((jax.random.randint(seeds[7], (TILES, LEVELS), 0, 4) < 3).astype(jnp.int32), jax.random.fold_in(seeds[7], 1), 0, 1),
    }


def pick_sampled(rows_block, onehot):
    grouped = rows_block.reshape(rows_block.shape[0] // RATE, RATE, rows_block.shape[1], rows_block.shape[2])
    return lax.optimization_barrier(jnp.sum(jnp.where(onehot[None, :, :, None], grouped, jnp.zeros_like(grouped)), axis=1))

def pick_segment(seg_block, onehot):
    grouped = seg_block.reshape(seg_block.shape[0] // RATE, RATE)
    picked = jnp.where(onehot[None, :, :], grouped[:, :, None], jnp.zeros((1, 1, 1), jnp.int32))
    return lax.optimization_barrier(jnp.sum(picked, axis=1)).astype(jnp.int32)

def reference(queries, key_rows, value_rows, out_grad, norm_gain, offsets, segments, tile_mask):
    score_scale = DH ** (-0.5)
    onehot_all = jnp.arange(RATE, dtype=jnp.int32)[None, :, None] == offsets[:, None, :]
    gain32 = norm_gain.astype(jnp.float32)
    tiles_dev = TOK_DEV // TILE

    def rows_of(array, first):
        return lax.dynamic_slice_in_dim(array, first, TOK_DEV, 0)

    def per_device(dev_index):
        start = (dev_index * TOK_DEV).astype(jnp.int32)
        query_blk = rows_of(queries, start).reshape(TOK_DEV, H, DH)
        key_blk = rows_of(key_rows, start).reshape(TOK_DEV, H, DH)
        value_blk = rows_of(value_rows, start).reshape(TOK_DEV, H, DH)
        grad_blk = rows_of(out_grad, start)
        seg_own = rows_of(segments, start)
        tile_rows = jnp.repeat(lax.dynamic_slice_in_dim(tile_mask, (dev_index * tiles_dev).astype(jnp.int32), tiles_dev, 0), TILE, axis=0)
        key_parts = [key_blk.transpose(1, 0, 2)]
        value_parts = [value_blk.transpose(1, 0, 2)]
        same_local = seg_own[:, None] == seg_own[None, :]
        allow_parts = [jnp.broadcast_to(same_local[None], (H, TOK_DEV, TOK_DEV))]
        for level_idx in range(LEVELS):
            partner = jnp.bitwise_xor(dev_index, 1 << level_idx).astype(jnp.int32)
            far_start = (partner * TOK_DEV).astype(jnp.int32)
            onehot = onehot_all[level_idx]
            key_parts.append(pick_sampled(rows_of(key_rows, far_start).reshape(TOK_DEV, H, DH), onehot).transpose(1, 0, 2))
            value_parts.append(pick_sampled(rows_of(value_rows, far_start).reshape(TOK_DEV, H, DH), onehot).transpose(1, 0, 2))
            seg_far = pick_segment(rows_of(segments, far_start), onehot)
            allow = (seg_own[None, :, None] == seg_far.T[:, None, :]) & (tile_rows[None, :, level_idx, None] == 1)
            allow_parts.append(allow)
        key_all = jnp.concatenate(key_parts, axis=1).astype(jnp.float32)
        value_all = jnp.concatenate(value_parts, axis=1).astype(jnp.float32)
        allowed = jnp.concatenate(allow_parts, axis=2)
        query32 = query_blk.astype(jnp.float32)
        logits = jnp.einsum('qhd,hkd->hqk', query32, key_all) * score_scale
        logits = jnp.where(allowed, logits, -1e+30)
        top = lax.optimization_barrier(jnp.max(logits, axis=-1, keepdims=True))
        expo = jnp.where(allowed, jnp.exp(logits - top), 0.0)
        weights = expo / lax.optimization_barrier(jnp.sum(expo, axis=-1, keepdims=True))
        weights_b = lax.optimization_barrier(weights.astype(jnp.bfloat16)).astype(jnp.float32)
        attended = jnp.einsum('hqk,hkd->qhd', weights_b, value_all).reshape(TOK_DEV, D)
        inv_rms = lax.rsqrt(lax.optimization_barrier(jnp.mean(attended * attended, axis=1)) + 1e-06)
        normed = (attended * inv_rms[:, None] * gain32).astype(jnp.bfloat16)
        scaled_grad = grad_blk.astype(jnp.float32) * gain32
        coupling = lax.optimization_barrier(jnp.mean(scaled_grad * attended, axis=1))
        grad_att = inv_rms[:, None] * (scaled_grad - attended * (inv_rms * inv_rms * coupling)[:, None])
        grad_att = lax.optimization_barrier(grad_att.astype(jnp.bfloat16)).astype(jnp.float32).reshape(TOK_DEV, H, DH)
        grad_w = jnp.einsum('qhd,hkd->hqk', grad_att, value_all)
        row_delta = lax.optimization_barrier(jnp.sum(weights * grad_w, axis=-1, keepdims=True))
        grad_logit = lax.optimization_barrier((weights * (grad_w - row_delta)).astype(jnp.bfloat16)).astype(jnp.float32)
        grad_q = (jnp.einsum('hqk,hkd->qhd', grad_logit, key_all) * score_scale).reshape(TOK_DEV, D).astype(jnp.bfloat16)
        key_term = jnp.einsum('hqk,qhd->hkd', grad_logit, query32) * score_scale
        value_term = jnp.einsum('hqk,qhd->hkd', weights_b, grad_att)
        local_k = key_term[:, :TOK_DEV].transpose(1, 0, 2)
        local_v = value_term[:, :TOK_DEV].transpose(1, 0, 2)
        far_k = key_term[:, TOK_DEV:].reshape(H, LEVELS, SAMPLED, DH).transpose(1, 2, 0, 3)
        far_v = value_term[:, TOK_DEV:].reshape(H, LEVELS, SAMPLED, DH).transpose(1, 2, 0, 3)
        return (normed, grad_q, local_k, local_v, far_k, far_v)
    normed, grad_q, local_k, local_v, far_k, far_v = lax.map(per_device, jnp.arange(N_CTX, dtype=jnp.int32))
    devices = jnp.arange(N_CTX, dtype=jnp.int32)
    total_k = local_k
    total_v = local_v
    for level_idx in range(LEVELS):
        partner = jnp.bitwise_xor(devices, 1 << level_idx).astype(jnp.int32)
        picker = onehot_all[level_idx][None, None, :, :, None]
        incoming_k = far_k[partner, level_idx]
        incoming_v = far_v[partner, level_idx]
        total_k = total_k + jnp.where(picker, incoming_k[:, :, None], 0.0).reshape(N_CTX, TOK_DEV, H, DH)
        total_v = total_v + jnp.where(picker, incoming_v[:, :, None], 0.0).reshape(N_CTX, TOK_DEV, H, DH)
    return (normed.reshape(TOKENS, D), grad_q.reshape(TOKENS, D), total_k.reshape(TOKENS, D).astype(jnp.bfloat16), total_v.reshape(TOKENS, D).astype(jnp.bfloat16))
```

```python
import functools

import jax
import jax.numpy as jnp
from jax import lax
from jax.experimental import pallas as pl
from jax.experimental.pallas import tpu as pltpu
from jax.sharding import PartitionSpec as P

DH = 128
RATE = 8
LEVELS = 3
LANES = 128
BIG = 1e30
EPS = 1e-06
TQ = 256
F32 = jnp.float32
BF16 = jnp.bfloat16
SCALE = DH ** (-0.5)
EXP2_SCALE = SCALE * 1.4426950408889634


def partner(value, axis, bit):
    mask = 2**bit
    pairs = [(source, source ^ mask) for source in range(lax.axis_size(axis))]
    return lax.ppermute(value, axis, pairs)


def dot_nt(a, b):
    return lax.dot_general(a, b, (((1,), (1,)), ((), ())), preferred_element_type=F32)


def dot_nn(a, b):
    return lax.dot_general(a, b, (((1,), (0,)), ((), ())), preferred_element_type=F32)


def dot_tn(a, b):
    return lax.dot_general(a, b, (((0,), (0,)), ((), ())), preferred_element_type=F32)


def lane_of(shape):
    return lax.broadcasted_iota(jnp.int32, shape, 1)


def column(tile, index):
    return jnp.sum(jnp.where(lane_of(tile.shape) == index, tile, 0.0), axis=1, keepdims=True)


def sample_kernel(off_ref, k_ref, v_ref, *rest):
    outs, (k_scr, v_scr) = rest[:-2], rest[-2:]
    head = pl.program_id(0)
    picks = k_ref.shape[0] // RATE
    k_scr[...] = k_ref[...].astype(F32)
    v_scr[...] = v_ref[...].astype(F32)
    for level, out in enumerate(outs):
        start = off_ref[level, head]
        out[0] = k_scr[pl.ds(start, picks, stride=RATE), :].astype(BF16)
        out[1] = v_scr[pl.ds(start, picks, stride=RATE), :].astype(BF16)


def forward_near_kernel(heads, q_ref, k_ref, v_ref, qf_ref, kf_ref, e_ref, acc_ref, stat_ref):
    head = pl.program_id(0)
    rows = q_ref.shape[0]
    key_aug = jnp.concatenate([k_ref[...], kf_ref[...]], axis=1)
    value_aug = jnp.concatenate([v_ref[...], jnp.ones((rows, LANES), BF16)], axis=1)
    for start in range(0, rows, TQ):
        part = pl.ds(start, TQ)
        query_aug = jnp.concatenate([q_ref[part, :], qf_ref[part, :]], axis=1)
        logits = dot_nt(query_aug, key_aug)
        top = jnp.max(logits, axis=1, keepdims=True)
        expo = jnp.exp2((logits - top) * EXP2_SCALE).astype(BF16)
        e_ref[0, part, :] = expo
        mixed = dot_nn(expo, value_aug)
        acc_ref[part, :] = mixed[:, :DH]
        lane = lane_of((TQ, LANES))
        kept = jnp.where(lane == head + heads, mixed[:, DH:], stat_ref[part, :])
        stat_ref[part, :] = jnp.where(lane == head, top, kept)


def forward_far_kernel(heads, levels, q_ref, qf_ref, ff_ref, acc_ref, stat_ref, og_ref, gain_ref, *rest):
    recv = rest[:levels]
    att_ref, ef_ref, rate_ref, sums_ref, ss_scr, sa_scr = rest[levels:]
    head = pl.program_id(0)
    rows = q_ref.shape[0]
    keys = jnp.concatenate([ref[0] for ref in recv], axis=0)
    values = jnp.concatenate([ref[1] for ref in recv], axis=0)
    key_aug = jnp.concatenate([keys, ff_ref[0]], axis=1)
    value_aug = jnp.concatenate([values, jnp.ones(values.shape, BF16)], axis=1)

    @pl.when(head == 0)
    def _():
        ss_scr[...] = jnp.zeros_like(ss_scr)
        sa_scr[...] = jnp.zeros_like(sa_scr)

    for start in range(0, rows, TQ):
        part = pl.ds(start, TQ)
        query_aug = jnp.concatenate([q_ref[part, :], qf_ref[part, :]], axis=1)
        logits = dot_nt(query_aug, key_aug)
        top_far = jnp.max(logits, axis=1, keepdims=True)
        expo = jnp.exp2((logits - top_far) * EXP2_SCALE).astype(BF16)
        ef_ref[0, part, :] = expo
        mixed = dot_nn(expo, value_aug)
        stat = stat_ref[part, :]
        top_near = column(stat, head)
        sum_near = column(stat, head + heads)
        top = jnp.maximum(top_near, top_far)
        a_near = jnp.exp2((top_near - top) * EXP2_SCALE)
        a_far = jnp.exp2((top_far - top) * EXP2_SCALE)
        inv = 1.0 / (a_near * sum_near + a_far * mixed[:, DH : DH + 1])
        r_near = a_near * inv
        r_far = a_far * inv
        att = r_near * acc_ref[part, :] + r_far * mixed[:, :DH]
        att_ref[part, :] = att
        lane = lane_of((TQ, LANES))
        kept = jnp.where(lane == head + heads, r_far, rate_ref[part, :])
        rate_ref[part, :] = jnp.where(lane == head, r_near, kept)
        scaled = og_ref[part, :].astype(F32) * gain_ref[...]
        ss_scr[part, :] += att * att
        sa_scr[part, :] += scaled * att

    @pl.when(head == pl.num_programs(0) - 1)
    def _():
        sums_ref[0:1, :] = jnp.sum(ss_scr[...].T, axis=0, keepdims=True)
        sums_ref[1:2, :] = jnp.sum(sa_scr[...].T, axis=0, keepdims=True)


def backward_far_kernel(heads, levels, width, att_ref, og_ref, gain_ref, sums_ref, rate_ref, q_ref, ef_ref, *rest):
    recv = rest[:levels]
    normed_ref, ga_ref, delta_ref, dq_ref = rest[levels : levels + 4]
    outs = rest[levels + 4 : levels + 4 + levels]
    inv_scr, cc_scr, gf_scr, gl_scr = rest[levels + 4 + levels :]
    head = pl.program_id(0)
    rows = q_ref.shape[0]
    picks = rows // RATE

    @pl.when(head == 0)
    def _():
        inv_row = lax.rsqrt(sums_ref[0:1, :] / width + EPS)
        cc_row = inv_row * inv_row * (sums_ref[1:2, :] / width)
        inv_scr[...] = jnp.broadcast_to(inv_row, (LANES, rows)).T
        cc_scr[...] = jnp.broadcast_to(cc_row, (LANES, rows)).T

    keys = jnp.concatenate([ref[0] for ref in recv], axis=0)
    values = jnp.concatenate([ref[1] for ref in recv], axis=0)
    gain = gain_ref[...]
    for start in range(0, rows, TQ):
        part = pl.ds(start, TQ)
        att = att_ref[part, :]
        inv = inv_scr[part, :]
        normed_ref[part, :] = (att * inv * gain).astype(BF16)
        scaled = og_ref[part, :].astype(F32) * gain
        grad_att = inv * (scaled - att * cc_scr[part, :])
        rate = rate_ref[part, :]
        ga_near = (grad_att * column(rate, head)).astype(BF16)
        ga_far = (grad_att * column(rate, head + heads)).astype(BF16)
        ga_ref[part, :] = ga_near
        gf_scr[part, :] = ga_far
        delta_near = jnp.sum(ga_near.astype(F32) * att, axis=1, keepdims=True)
        delta_far = jnp.sum(ga_far.astype(F32) * att, axis=1, keepdims=True)
        lane = lane_of((TQ, LANES))
        delta_ref[part, :] = jnp.where(lane == head, delta_near, delta_ref[part, :])
        grad_w = dot_nt(ga_far, values)
        expo = ef_ref[0, part, :]
        gl = (expo.astype(F32) * (grad_w - delta_far)).astype(BF16)
        gl_scr[part, :] = gl
        dq_ref[part, :] = dot_nn(gl, keys)
    dk = dot_tn(gl_scr[...], q_ref[...]) * SCALE
    dv = dot_tn(ef_ref[0], gf_scr[...])
    for level, out in enumerate(outs):
        out[0] = dk[level * picks : (level + 1) * picks].astype(BF16)
        out[1] = dv[level * picks : (level + 1) * picks].astype(BF16)


def backward_near_kernel(e_ref, ga_ref, delta_ref, q_ref, k_ref, v_ref, dqf_ref, dq_ref, dk_ref, dv_ref, gl_scr):
    head = pl.program_id(0)
    rows = q_ref.shape[0]
    for start in range(0, rows, TQ):
        part = pl.ds(start, TQ)
        grad_w = dot_nt(ga_ref[part, :], v_ref[...])
        delta = column(delta_ref[part, :], head)
        gl = (e_ref[0, part, :].astype(F32) * (grad_w - delta)).astype(BF16)
        gl_scr[part, :] = gl
        dq_ref[part, :] = ((dot_nn(gl, k_ref[...]) + dqf_ref[part, :]) * SCALE).astype(BF16)
    dk_ref[...] = dot_tn(gl_scr[...], q_ref[...]) * SCALE
    dv_ref[...] = dot_tn(e_ref[0], ga_ref[...])


def merge_kernel(levels, off_ref, dk_ref, dv_ref, *rest):
    back = rest[:levels]
    gk_ref, gv_ref, k_scr, v_scr = rest[levels:]
    head = pl.program_id(0)
    picks = dk_ref.shape[0] // RATE
    k_scr[...] = dk_ref[...]
    v_scr[...] = dv_ref[...]
    for level in range(levels):
        spot = pl.ds(off_ref[level, head], picks, stride=RATE)
        k_scr[spot, :] += back[level][0].astype(F32)
        v_scr[spot, :] += back[level][1].astype(F32)
    gk_ref[...] = k_scr[...].astype(BF16)
    gv_ref[...] = v_scr[...].astype(BF16)


def local(queries, key_rows, value_rows, out_grad, norm_gain, offsets, segments, tile_mask):
    rows, width = queries.shape
    heads = width // DH
    picks = rows // RATE
    total_width = width * lax.axis_size("head")
    own = lax.axis_index("ctx")
    tile = rows // tile_mask.shape[0]

    by_head = pl.BlockSpec((rows, DH), lambda h: (0, h))
    whole = pl.BlockSpec((rows, LANES), lambda h: (0, 0))
    pair = pl.BlockSpec((2, picks, DH), lambda h: (0, 0, h))
    smem = pl.BlockSpec(memory_space=pltpu.SMEM)
    gain_row = norm_gain.reshape(1, width)
    gain_spec = pl.BlockSpec((1, DH), lambda h: (0, h))
    params = pltpu.CompilerParams(dimension_semantics=("arbitrary",), vmem_limit_bytes=60 << 20)

    def call(kernel, name, in_specs, out_specs, out_shape, scratch=(), flops=0, moved=0, expo=0):
        return pl.pallas_call(
            kernel,
            name=name,
            grid=(heads,),
            in_specs=in_specs,
            out_specs=out_specs,
            out_shape=out_shape,
            scratch_shapes=scratch,
            compiler_params=params,
            cost_estimate=pl.CostEstimate(flops=flops, bytes_accessed=moved, transcendentals=expo),
        )

    def shape(dims, dtype):
        return jax.ShapeDtypeStruct(dims, dtype)

    full = rows * width
    pair_shape = shape((2, picks, width), BF16)
    samples = call(
        sample_kernel,
        "sample",
        [smem, by_head, by_head],
        [pair] * LEVELS,
        [pair_shape] * LEVELS,
        [pltpu.VMEM((rows, DH), F32)] * 2,
        moved=4 * full,
    )(offsets, key_rows, value_rows)
    recv = [partner(samples[level], "ctx", level) for level in range(LEVELS)]

    lane = jnp.arange(LANES, dtype=jnp.int32)[None, :]
    seg_own = lax.dynamic_slice_in_dim(segments, own * rows, rows, 0)
    same = seg_own[:, None] == lane
    closed = jnp.repeat(tile_mask, tile, axis=0) != 1
    query_feat = same.astype(BF16)
    for level in range(LEVELS):
        hit = (lane == LANES - 1 - level) & closed[:, level : level + 1]
        query_feat = jnp.where(hit, jnp.ones((), BF16), query_feat)
    key_feat = jnp.where(same | (lane >= LANES - LEVELS), 0.0, -BIG).astype(BF16)
    far_feats = []
    for level in range(LEVELS):
        far_start = jnp.bitwise_xor(own, 2**level) * rows
        seg_far = lax.dynamic_slice_in_dim(segments, far_start, rows, 0).reshape(picks, RATE)
        onehot = jnp.arange(RATE, dtype=jnp.int32)[:, None] == offsets[level][None, :]
        picked = jnp.sum(jnp.where(onehot[None], seg_far[:, :, None], 0), axis=1)
        blocked = (picked.T[:, :, None] != lane[None]) & (lane[None] < LANES - LEVELS)
        blocked = blocked | (lane[None] == LANES - 1 - level)
        far_feats.append(jnp.where(blocked, -BIG, 0.0).astype(BF16))
    far_feat = jnp.concatenate(far_feats, axis=1)

    square = rows * rows * heads
    expo, acc, stat = call(
        functools.partial(forward_near_kernel, heads),
        "forward_near",
        [by_head, by_head, by_head, whole, whole],
        [pl.BlockSpec((1, rows, rows), lambda h: (h, 0, 0)), by_head, whole],
        [shape((heads, rows, rows), BF16), shape((rows, width), F32), shape((rows, LANES), F32)],
        flops=4 * square * DH,
        moved=2 * square + 10 * full,
        expo=square,
    )(queries, key_rows, value_rows, query_feat, key_feat)

    far_n = LEVELS * picks
    far_spec = pl.BlockSpec((1, rows, far_n), lambda h: (h, 0, 0))
    far_square = rows * far_n * heads
    att, expo_far, rate, sums = call(
        functools.partial(forward_far_kernel, heads, LEVELS),
        "forward_far",
        [by_head, whole, pl.BlockSpec((1, far_n, LANES), lambda h: (h, 0, 0)), by_head, whole, by_head, gain_spec]
        + [pair] * LEVELS,
        [by_head, far_spec, whole, pl.BlockSpec((2, rows), lambda h: (0, 0))],
        [shape((rows, width), F32), shape((heads, rows, far_n), BF16), shape((rows, LANES), F32), shape((2, rows), F32)],
        [pltpu.VMEM((rows, LANES), F32)] * 2,
        flops=4 * far_square * DH,
        moved=2 * far_square + 12 * full,
        expo=far_square,
    )(queries, query_feat, far_feat, acc, stat, out_grad, gain_row, *recv)
    sums = lax.psum(sums, "head")

    outs = call(
        functools.partial(backward_far_kernel, heads, LEVELS, total_width),
        "backward_far",
        [by_head, by_head, gain_spec, pl.BlockSpec((2, rows), lambda h: (0, 0)), whole, by_head, far_spec]
        + [pair] * LEVELS,
        [by_head, by_head, whole, by_head] + [pair] * LEVELS,
        [shape((rows, width), BF16), shape((rows, width), BF16), shape((rows, LANES), F32), shape((rows, width), F32)]
        + [pair_shape] * LEVELS,
        [
            pltpu.VMEM((rows, LANES), F32),
            pltpu.VMEM((rows, LANES), F32),
            pltpu.VMEM((rows, DH), BF16),
            pltpu.VMEM((rows, far_n), BF16),
        ],
        flops=8 * far_square * DH,
        moved=2 * far_square + 16 * full,
    )(att, out_grad, gain_row, sums, rate, queries, expo_far, *recv)
    normed, grad_att, delta, dq_far = outs[:4]
    back = [partner(outs[4 + level], "ctx", level) for level in range(LEVELS)]

    grad_queries, dk, dv = call(
        backward_near_kernel,
        "backward_near",
        [pl.BlockSpec((1, rows, rows), lambda h: (h, 0, 0)), by_head, whole, by_head, by_head, by_head, by_head],
        [by_head, by_head, by_head],
        [shape((rows, width), BF16), shape((rows, width), F32), shape((rows, width), F32)],
        [pltpu.VMEM((rows, rows), BF16)],
        flops=8 * square * DH,
        moved=2 * square + 22 * full,
    )(expo, grad_att, delta, queries, key_rows, value_rows, dq_far)

    grad_keys, grad_values = call(
        functools.partial(merge_kernel, LEVELS),
        "merge",
        [smem, by_head, by_head] + [pair] * LEVELS,
        [by_head, by_head],
        [shape((rows, width), BF16)] * 2,
        [pltpu.VMEM((rows, DH), F32)] * 2,
        moved=14 * full,
    )(offsets, dk, dv, *back)
    return (normed, grad_queries, grad_keys, grad_values)


def solution(mesh):
    placed = (
        P("ctx", "head"),
        P("ctx", "head"),
        P("ctx", "head"),
        P("ctx", "head"),
        P("head"),
        P(None, "head"),
        P(),
        P("ctx", None),
    )
    return jax.shard_map(
        local,
        mesh=mesh,
        in_specs=placed,
        out_specs=(P("ctx", "head"), P("ctx", "head"), P("ctx", "head"), P("ctx", "head")),
        check_vma=False,
    )
```

```python
import functools

import jax
import jax.numpy as jnp
from jax import lax
from jax.experimental import pallas as pl
from jax.experimental.pallas import tpu as pltpu
from jax.sharding import PartitionSpec as P

DH = 128
RATE = 8
LEVELS = 3
LANES = 128
BIG = 1e30
EPS = 1e-06
TQ = 256
F32 = jnp.float32
BF16 = jnp.bfloat16
SCALE = DH ** (-0.5)
EXP2_SCALE = SCALE * 1.4426950408889634


def partner(value, axis, bit):
    mask = 2**bit
    pairs = [(source, source ^ mask) for source in range(lax.axis_size(axis))]
    return lax.ppermute(value, axis, pairs)


def dot_nt(a, b):
    return lax.dot_general(a, b, (((1,), (1,)), ((), ())), preferred_element_type=F32)


def dot_nn(a, b):
    return lax.dot_general(a, b, (((1,), (0,)), ((), ())), preferred_element_type=F32)


def dot_tn(a, b):
    return lax.dot_general(a, b, (((0,), (0,)), ((), ())), preferred_element_type=F32)


def lane_of(shape):
    return lax.broadcasted_iota(jnp.int32, shape, 1)


def column(tile, index):
    return jnp.sum(jnp.where(lane_of(tile.shape) == index, tile, 0.0), axis=1, keepdims=True)


def sample_kernel(off_ref, k_ref, v_ref, *rest):
    outs, (k_scr, v_scr) = rest[:-2], rest[-2:]
    head = pl.program_id(0)
    picks = k_ref.shape[0] // RATE
    k_scr[...] = k_ref[...].astype(F32)
    v_scr[...] = v_ref[...].astype(F32)
    for level, out in enumerate(outs):
        start = off_ref[level, head]
        out[0] = k_scr[pl.ds(start, picks, stride=RATE), :].astype(BF16)
        out[1] = v_scr[pl.ds(start, picks, stride=RATE), :].astype(BF16)


def forward_near_kernel(heads, q_ref, k_ref, v_ref, qf_ref, kf_ref, e_ref, acc_ref, stat_ref):
    head = pl.program_id(0)
    rows = q_ref.shape[0]
    key_aug = jnp.concatenate([k_ref[...], kf_ref[...]], axis=1)
    value_aug = jnp.concatenate([v_ref[...], jnp.ones((rows, LANES), BF16)], axis=1)
    for start in range(0, rows, TQ):
        part = pl.ds(start, TQ)
        query_aug = jnp.concatenate([q_ref[part, :], qf_ref[part, :]], axis=1)
        logits = dot_nt(query_aug, key_aug)
        top = jnp.max(logits, axis=1, keepdims=True)
        expo = jnp.exp2((logits - top) * EXP2_SCALE).astype(BF16)
        e_ref[0, part, :] = expo
        mixed = dot_nn(expo, value_aug)
        acc_ref[part, :] = mixed[:, :DH]
        lane = lane_of((TQ, LANES))
        kept = jnp.where(lane == head + heads, mixed[:, DH:], stat_ref[part, :])
        stat_ref[part, :] = jnp.where(lane == head, top, kept)


def forward_far_kernel(heads, levels, q_ref, qf_ref, ff_ref, acc_ref, stat_ref, og_ref, gain_ref, *rest):
    recv = rest[:levels]
    att_ref, ef_ref, rate_ref, sums_ref, ss_scr, sa_scr = rest[levels:]
    head = pl.program_id(0)
    rows = q_ref.shape[0]
    keys = jnp.concatenate([ref[0] for ref in recv], axis=0)
    values = jnp.concatenate([ref[1] for ref in recv], axis=0)
    key_aug = jnp.concatenate([keys, ff_ref[0]], axis=1)
    value_aug = jnp.concatenate([values, jnp.ones(values.shape, BF16)], axis=1)

    @pl.when(head == 0)
    def _():
        ss_scr[...] = jnp.zeros_like(ss_scr)
        sa_scr[...] = jnp.zeros_like(sa_scr)

    for start in range(0, rows, TQ):
        part = pl.ds(start, TQ)
        query_aug = jnp.concatenate([q_ref[part, :], qf_ref[part, :]], axis=1)
        logits = dot_nt(query_aug, key_aug)
        top_far = jnp.max(logits, axis=1, keepdims=True)
        expo = jnp.exp2((logits - top_far) * EXP2_SCALE).astype(BF16)
        ef_ref[0, part, :] = expo
        mixed = dot_nn(expo, value_aug)
        stat = stat_ref[part, :]
        top_near = column(stat, head)
        sum_near = column(stat, head + heads)
        top = jnp.maximum(top_near, top_far)
        a_near = jnp.exp2((top_near - top) * EXP2_SCALE)
        a_far = jnp.exp2((top_far - top) * EXP2_SCALE)
        inv = 1.0 / (a_near * sum_near + a_far * mixed[:, DH : DH + 1])
        r_near = a_near * inv
        r_far = a_far * inv
        att = r_near * acc_ref[part, :] + r_far * mixed[:, :DH]
        att_ref[part, :] = att
        lane = lane_of((TQ, LANES))
        kept = jnp.where(lane == head + heads, r_far, rate_ref[part, :])
        rate_ref[part, :] = jnp.where(lane == head, r_near, kept)
        scaled = og_ref[part, :].astype(F32) * gain_ref[...]
        ss_scr[part, :] += att * att
        sa_scr[part, :] += scaled * att

    @pl.when(head == pl.num_programs(0) - 1)
    def _():
        sums_ref[0:1, :] = jnp.sum(ss_scr[...].T, axis=0, keepdims=True)
        sums_ref[1:2, :] = jnp.sum(sa_scr[...].T, axis=0, keepdims=True)


def backward_far_kernel(heads, levels, width, parts, *refs):
    gathered = refs[:parts]
    att_ref, og_ref, gain_ref, rate_ref, q_ref, ef_ref = refs[parts : parts + 6]
    rest = refs[parts + 6 :]
    recv = rest[:levels]
    normed_ref, ga_ref, delta_ref, dq_ref = rest[levels : levels + 4]
    outs = rest[levels + 4 : levels + 4 + levels]
    inv_scr, cc_scr, gf_scr, gl_scr = rest[levels + 4 + levels :]
    head = pl.program_id(0)
    rows = q_ref.shape[0]
    picks = rows // RATE

    @pl.when(head == 0)
    def _():
        sums = functools.reduce(jnp.add, [ref[...] for ref in gathered])
        inv_row = lax.rsqrt(sums[0:1, :] / width + EPS)
        cc_row = inv_row * inv_row * (sums[1:2, :] / width)
        inv_scr[...] = jnp.broadcast_to(inv_row, (LANES, rows)).T
        cc_scr[...] = jnp.broadcast_to(cc_row, (LANES, rows)).T

    keys = jnp.concatenate([ref[0] for ref in recv], axis=0)
    values = jnp.concatenate([ref[1] for ref in recv], axis=0)
    gain = gain_ref[...]
    for start in range(0, rows, TQ):
        part = pl.ds(start, TQ)
        att = att_ref[part, :]
        inv = inv_scr[part, :]
        normed_ref[part, :] = (att * inv * gain).astype(BF16)
        scaled = og_ref[part, :].astype(F32) * gain
        grad_att = inv * (scaled - att * cc_scr[part, :])
        rate = rate_ref[part, :]
        ga_near = (grad_att * column(rate, head)).astype(BF16)
        ga_far = (grad_att * column(rate, head + heads)).astype(BF16)
        ga_ref[part, :] = ga_near
        gf_scr[part, :] = ga_far
        delta_near = jnp.sum(ga_near.astype(F32) * att, axis=1, keepdims=True)
        delta_far = jnp.sum(ga_far.astype(F32) * att, axis=1, keepdims=True)
        lane = lane_of((TQ, LANES))
        delta_ref[part, :] = jnp.where(lane == head, delta_near, delta_ref[part, :])
        grad_w = dot_nt(ga_far, values)
        expo = ef_ref[0, part, :]
        gl = (expo.astype(F32) * (grad_w - delta_far)).astype(BF16)
        gl_scr[part, :] = gl
        dq_ref[part, :] = dot_nn(gl, keys)
    dk = dot_tn(gl_scr[...], q_ref[...]) * SCALE
    dv = dot_tn(ef_ref[0], gf_scr[...])
    for level, out in enumerate(outs):
        out[0] = dk[level * picks : (level + 1) * picks].astype(BF16)
        out[1] = dv[level * picks : (level + 1) * picks].astype(BF16)


def backward_near_kernel(e_ref, ga_ref, delta_ref, q_ref, k_ref, v_ref, dqf_ref, dq_ref, dk_ref, dv_ref, gl_scr):
    head = pl.program_id(0)
    rows = q_ref.shape[0]
    for start in range(0, rows, TQ):
        part = pl.ds(start, TQ)
        grad_w = dot_nt(ga_ref[part, :], v_ref[...])
        delta = column(delta_ref[part, :], head)
        gl = (e_ref[0, part, :].astype(F32) * (grad_w - delta)).astype(BF16)
        gl_scr[part, :] = gl
        dq_ref[part, :] = ((dot_nn(gl, k_ref[...]) + dqf_ref[part, :]) * SCALE).astype(BF16)
    dk_ref[...] = dot_tn(gl_scr[...], q_ref[...]) * SCALE
    dv_ref[...] = dot_tn(e_ref[0], ga_ref[...])


def merge_kernel(levels, off_ref, dk_ref, dv_ref, *rest):
    back = rest[:levels]
    gk_ref, gv_ref, k_scr, v_scr = rest[levels:]
    head = pl.program_id(0)
    picks = dk_ref.shape[0] // RATE
    k_scr[...] = dk_ref[...]
    v_scr[...] = dv_ref[...]
    for level in range(levels):
        spot = pl.ds(off_ref[level, head], picks, stride=RATE)
        k_scr[spot, :] += back[level][0].astype(F32)
        v_scr[spot, :] += back[level][1].astype(F32)
    gk_ref[...] = k_scr[...].astype(BF16)
    gv_ref[...] = v_scr[...].astype(BF16)


def local(queries, key_rows, value_rows, out_grad, norm_gain, offsets, segments, tile_mask):
    rows, width = queries.shape
    heads = width // DH
    picks = rows // RATE
    total_width = width * lax.axis_size("head")
    own = lax.axis_index("ctx")
    tile = rows // tile_mask.shape[0]

    by_head = pl.BlockSpec((rows, DH), lambda h: (0, h))
    whole = pl.BlockSpec((rows, LANES), lambda h: (0, 0))
    pair = pl.BlockSpec((2, picks, DH), lambda h: (0, 0, h))
    smem = pl.BlockSpec(memory_space=pltpu.SMEM)
    gain_row = norm_gain.reshape(1, width)
    gain_spec = pl.BlockSpec((1, DH), lambda h: (0, h))

    def call(kernel, name, mib, in_specs, out_specs, out_shape, scratch=(), flops=0, moved=0, expo=0):
        return pl.pallas_call(
            kernel,
            name=name,
            grid=(heads,),
            in_specs=in_specs,
            out_specs=out_specs,
            out_shape=out_shape,
            scratch_shapes=scratch,
            compiler_params=pltpu.CompilerParams(dimension_semantics=("arbitrary",), vmem_limit_bytes=mib << 20),
            cost_estimate=pl.CostEstimate(flops=flops, bytes_accessed=moved, transcendentals=expo),
        )

    def shape(dims, dtype):
        return jax.ShapeDtypeStruct(dims, dtype)

    full = rows * width
    pair_shape = shape((2, picks, width), BF16)
    samples = call(
        sample_kernel,
        "sample",
        5,
        [smem, by_head, by_head],
        [pair] * LEVELS,
        [pair_shape] * LEVELS,
        [pltpu.VMEM((rows, DH), F32)] * 2,
        moved=4 * full,
    )(offsets, key_rows, value_rows)
    recv = [partner(samples[level], "ctx", level) for level in range(LEVELS)]

    lane = jnp.arange(LANES, dtype=jnp.int32)[None, :]
    seg_own = lax.dynamic_slice_in_dim(segments, own * rows, rows, 0)
    same = seg_own[:, None] == lane
    closed = jnp.repeat(tile_mask, tile, axis=0) != 1
    query_feat = same.astype(BF16)
    for level in range(LEVELS):
        hit = (lane == LANES - 1 - level) & closed[:, level : level + 1]
        query_feat = jnp.where(hit, jnp.ones((), BF16), query_feat)
    key_feat = jnp.where(same | (lane >= LANES - LEVELS), 0.0, -BIG).astype(BF16)
    far_feats = []
    for level in range(LEVELS):
        far_start = jnp.bitwise_xor(own, 2**level) * rows
        seg_far = lax.dynamic_slice_in_dim(segments, far_start, rows, 0).reshape(picks, RATE)
        onehot = jnp.arange(RATE, dtype=jnp.int32)[:, None] == offsets[level][None, :]
        picked = jnp.sum(jnp.where(onehot[None], seg_far[:, :, None], 0), axis=1)
        blocked = (picked.T[:, :, None] != lane[None]) & (lane[None] < LANES - LEVELS)
        blocked = blocked | (lane[None] == LANES - 1 - level)
        far_feats.append(jnp.where(blocked, -BIG, 0.0).astype(BF16))
    far_feat = jnp.concatenate(far_feats, axis=1)

    square = rows * rows * heads
    expo, acc, stat = call(
        functools.partial(forward_near_kernel, heads),
        "forward_near",
        12,
        [by_head, by_head, by_head, whole, whole],
        [pl.BlockSpec((1, rows, rows), lambda h: (h, 0, 0)), by_head, whole],
        [pltpu.HBM((heads, rows, rows), BF16), shape((rows, width), F32), shape((rows, LANES), F32)],
        flops=4 * square * DH,
        moved=2 * square + 10 * full,
        expo=square,
    )(queries, key_rows, value_rows, query_feat, key_feat)

    far_n = LEVELS * picks
    far_spec = pl.BlockSpec((1, rows, far_n), lambda h: (h, 0, 0))
    far_square = rows * far_n * heads
    att, expo_far, rate, sums = call(
        functools.partial(forward_far_kernel, heads, LEVELS),
        "forward_far",
        10,
        [by_head, whole, pl.BlockSpec((1, far_n, LANES), lambda h: (h, 0, 0)), by_head, whole, by_head, gain_spec]
        + [pair] * LEVELS,
        [by_head, far_spec, whole, pl.BlockSpec((2, rows), lambda h: (0, 0))],
        [shape((rows, width), F32), shape((heads, rows, far_n), BF16), shape((rows, LANES), F32), shape((2, rows), F32)],
        [pltpu.VMEM((rows, LANES), F32)] * 2,
        flops=4 * far_square * DH,
        moved=2 * far_square + 12 * full,
        expo=far_square,
    )(queries, query_feat, far_feat, acc, stat, out_grad, gain_row, *recv)
    parts = lax.axis_size("head")
    shifted = [
        lax.ppermute(sums, "head", [(i, (i + step) % parts) for i in range(parts)]) for step in range(1, parts)
    ]
    gathered = [sums] + shifted

    outs = call(
        functools.partial(backward_far_kernel, heads, LEVELS, total_width, parts),
        "backward_far",
        10,
        [pl.BlockSpec((2, rows), lambda h: (0, 0))] * parts
        + [by_head, by_head, gain_spec, whole, by_head, far_spec]
        + [pair] * LEVELS,
        [by_head, by_head, whole, by_head] + [pair] * LEVELS,
        [shape((rows, width), BF16), shape((rows, width), BF16), shape((rows, LANES), F32), shape((rows, width), F32)]
        + [pair_shape] * LEVELS,
        [
            pltpu.VMEM((rows, LANES), F32),
            pltpu.VMEM((rows, LANES), F32),
            pltpu.VMEM((rows, DH), BF16),
            pltpu.VMEM((rows, far_n), BF16),
        ],
        flops=8 * far_square * DH,
        moved=2 * far_square + 16 * full,
    )(*gathered, att, out_grad, gain_row, rate, queries, expo_far, *recv)
    normed, grad_att, delta, dq_far = outs[:4]
    back = [partner(outs[4 + level], "ctx", level) for level in range(LEVELS)]

    grad_queries, dk, dv = call(
        backward_near_kernel,
        "backward_near",
        13,
        [pl.BlockSpec((1, rows, rows), lambda h: (h, 0, 0)), by_head, whole, by_head, by_head, by_head, by_head],
        [by_head, by_head, by_head],
        [shape((rows, width), BF16), shape((rows, width), F32), shape((rows, width), F32)],
        [pltpu.VMEM((rows, rows), BF16)],
        flops=8 * square * DH,
        moved=2 * square + 22 * full,
    )(pltpu.with_memory_space_constraint(expo, pltpu.HBM), grad_att, delta, queries, key_rows, value_rows, dq_far)

    grad_keys, grad_values = call(
        functools.partial(merge_kernel, LEVELS),
        "merge",
        7,
        [smem, by_head, by_head] + [pair] * LEVELS,
        [by_head, by_head],
        [shape((rows, width), BF16)] * 2,
        [pltpu.VMEM((rows, DH), F32)] * 2,
        moved=14 * full,
    )(offsets, dk, dv, *back)
    return (normed, grad_queries, grad_keys, grad_values)


def solution(mesh):
    placed = (
        P("ctx", "head"),
        P("ctx", "head"),
        P("ctx", "head"),
        P("ctx", "head"),
        P("head"),
        P(None, "head"),
        P(),
        P("ctx", None),
    )
    return jax.shard_map(
        local,
        mesh=mesh,
        in_specs=placed,
        out_specs=(P("ctx", "head"), P("ctx", "head"), P("ctx", "head"), P("ctx", "head")),
        check_vma=False,
    )
```

```python
import functools

import jax
import jax.numpy as jnp
from jax import lax
from jax.experimental import pallas as pl
from jax.experimental.pallas import tpu as pltpu
from jax.sharding import PartitionSpec as P

DH = 128
RATE = 8
LEVELS = 3
LANES = 128
BIG = 1e30
EPS = 1e-06
TQ = 256
F32 = jnp.float32
BF16 = jnp.bfloat16
SCALE = DH ** (-0.5)
EXP2_SCALE = SCALE * 1.4426950408889634


def partner(value, axis, bit):
    mask = 2**bit
    pairs = [(source, source ^ mask) for source in range(lax.axis_size(axis))]
    return lax.ppermute(value, axis, pairs)


def dot_nt(a, b):
    return lax.dot_general(a, b, (((1,), (1,)), ((), ())), preferred_element_type=F32)


def dot_nn(a, b):
    return lax.dot_general(a, b, (((1,), (0,)), ((), ())), preferred_element_type=F32)


def dot_tn(a, b):
    return lax.dot_general(a, b, (((0,), (0,)), ((), ())), preferred_element_type=F32)


def lane_of(shape):
    return lax.broadcasted_iota(jnp.int32, shape, 1)


def sample_kernel(off_ref, k_ref, v_ref, *rest):
    outs, (k_scr, v_scr) = rest[:-2], rest[-2:]
    head = pl.program_id(0)
    picks = k_ref.shape[0] // RATE
    k_scr[...] = k_ref[...].astype(F32)
    v_scr[...] = v_ref[...].astype(F32)
    for level, out in enumerate(outs):
        start = off_ref[level, head]
        out[0] = k_scr[pl.ds(start, picks, stride=RATE), :].astype(BF16)
        out[1] = v_scr[pl.ds(start, picks, stride=RATE), :].astype(BF16)


def as_columns(row):
    return jnp.broadcast_to(row, (LANES, row.shape[1])).T


def forward_near_kernel(heads, own_ref, q_ref, k_ref, v_ref, seg_ref, e_ref, acc_ref, stat_ref, va_scr, seg_scr, stat_scr):
    head = pl.program_id(0)
    rows = q_ref.shape[0]
    seg_row = seg_ref[pl.ds(own_ref[0], 1), :]

    @pl.when(head == 0)
    def _():
        va_scr[:, DH:] = jnp.ones((rows, LANES), BF16)
        seg_scr[...] = as_columns(seg_row)

    va_scr[:, :DH] = v_ref[...]
    for start in range(0, rows, TQ):
        part = pl.ds(start, TQ)
        logits = dot_nt(q_ref[part, :], k_ref[...])
        seg_col = jnp.concatenate([seg_scr[part, :]] * (rows // LANES), axis=1)
        logits = jnp.where(seg_col == seg_row, logits, -BIG)
        top = jnp.max(logits, axis=1, keepdims=True)
        expo = jnp.exp2((logits - top) * EXP2_SCALE).astype(BF16)
        e_ref[0, part, :] = expo
        mixed = dot_nn(expo, va_scr[...])
        acc_ref[part, :] = mixed[:, :DH]
        lane = lane_of((TQ, LANES))
        kept = jnp.where(lane == head + heads, mixed[:, DH:], stat_scr[part, :])
        stat_scr[part, :] = jnp.where(lane == head, top, kept)

    @pl.when(head == pl.num_programs(0) - 1)
    def _():
        stat_ref[...] = stat_scr[...].T[: 2 * heads, :]


def forward_far_kernel(heads, levels, own_ref, off_ref, mask_ref, q_ref, seg_ref, acc_ref, stat_ref, og_ref, gain_ref, *rest):
    recv = rest[:levels]
    att_ref, ef_ref, rate_ref, sums_ref, ss_scr, sa_scr, open_scr = rest[levels : levels + 7]
    seg_scr = rest[levels + 7 :]
    head = pl.program_id(0)
    rows = q_ref.shape[0]
    picks = rows // RATE
    tiles = mask_ref.shape[0]
    tile = rows // tiles
    keys = jnp.concatenate([ref[0] for ref in recv], axis=0)
    values = jnp.concatenate([ref[1] for ref in recv], axis=0)

    @pl.when(head == 0)
    def _():
        ss_scr[...] = jnp.zeros_like(ss_scr)
        sa_scr[...] = jnp.zeros_like(sa_scr)
        own = own_ref[0]
        own_row = seg_ref[pl.ds(own, 1), :]
        for level in range(levels):
            other = jnp.bitwise_xor(own, 2**level)
            seg_scr[level][...] = as_columns(seg_ref[pl.ds(other, 1), :])
            for index in range(tiles):
                span = slice(index * tile, (index + 1) * tile)
                shut = jnp.where(mask_ref[index, level] == 1, 0.0, 1.0)
                open_scr[level : level + 1, span] = own_row[:, span] - 1000.0 * shut

    allowed = []
    for level in range(levels):
        seg_col = seg_scr[level][pl.ds(off_ref[level, head], picks, stride=RATE), :]
        seg_col = jnp.concatenate([seg_col] * (rows // LANES), axis=1)
        allowed.append(seg_col == open_scr[level : level + 1, :])
    logits = dot_nt(keys, q_ref[...])
    logits = jnp.where(jnp.concatenate(allowed, axis=0), logits, -BIG)
    top_far = jnp.max(logits, axis=0, keepdims=True)
    expo = jnp.exp2((logits - top_far) * EXP2_SCALE).astype(BF16)
    ef_ref[0] = expo
    mixed = dot_tn(expo, values)
    sum_far = dot_nn(jnp.ones((16, expo.shape[0]), BF16), expo)[0:1, :]
    top_near = stat_ref[pl.ds(head, 1), :]
    sum_near = stat_ref[pl.ds(head + heads, 1), :]
    top = jnp.maximum(top_near, top_far)
    a_near = jnp.exp2((top_near - top) * EXP2_SCALE)
    a_far = jnp.exp2((top_far - top) * EXP2_SCALE)
    inv = 1.0 / (a_near * sum_near + a_far * sum_far)
    r_near = a_near * inv
    r_far = a_far * inv
    rate_ref[pl.ds(head, 1), :] = r_near
    rate_ref[pl.ds(head + heads, 1), :] = r_far
    att = as_columns(r_near) * acc_ref[...] + as_columns(r_far) * mixed
    att_ref[...] = att
    scaled = og_ref[...].astype(F32) * gain_ref[...]
    ss_scr[...] += att * att
    sa_scr[...] += scaled * att

    @pl.when(head == pl.num_programs(0) - 1)
    def _():
        sums_ref[0:1, :] = jnp.sum(ss_scr[...].T, axis=0, keepdims=True)
        sums_ref[1:2, :] = jnp.sum(sa_scr[...].T, axis=0, keepdims=True)


def backward_far_kernel(heads, levels, width, parts, *refs):
    gathered = refs[:parts]
    att_ref, og_ref, gain_ref, rate_ref, q_ref, ef_ref = refs[parts : parts + 6]
    rest = refs[parts + 6 :]
    recv = rest[:levels]
    normed_ref, ga_ref, delta_ref, dq_ref = rest[levels : levels + 4]
    outs = rest[levels + 4 : levels + 4 + levels]
    inv_scr, cc_scr = rest[levels + 4 + levels :]
    head = pl.program_id(0)
    rows = q_ref.shape[0]
    picks = rows // RATE

    @pl.when(head == 0)
    def _():
        sums = functools.reduce(jnp.add, [ref[...] for ref in gathered])
        inv_row = lax.rsqrt(sums[0:1, :] / width + EPS)
        inv_scr[...] = as_columns(inv_row)
        cc_scr[...] = as_columns(inv_row * inv_row * (sums[1:2, :] / width))

    keys = jnp.concatenate([ref[0] for ref in recv], axis=0)
    values = jnp.concatenate([ref[1] for ref in recv], axis=0)
    gain = gain_ref[...]
    att = att_ref[...]
    inv = inv_scr[...]
    normed_ref[...] = (att * inv * gain).astype(BF16)
    scaled = og_ref[...].astype(F32) * gain
    grad_att = inv * (scaled - att * cc_scr[...])
    ga_near = (grad_att * as_columns(rate_ref[pl.ds(head, 1), :])).astype(BF16)
    ga_far = (grad_att * as_columns(rate_ref[pl.ds(head + heads, 1), :])).astype(BF16)
    ga_ref[...] = ga_near
    delta_near = jnp.sum(ga_near.astype(F32) * att, axis=1, keepdims=True)
    delta_ref[...] = jnp.broadcast_to(delta_near, (rows, LANES))
    delta_far = jnp.sum((ga_far.astype(F32) * att).T, axis=0, keepdims=True)
    grad_w = dot_nt(values, ga_far)
    expo = ef_ref[0]
    gl = (expo.astype(F32) * (grad_w - delta_far)).astype(BF16)
    dq_ref[...] = dot_tn(gl, keys)
    dk = dot_nn(gl, q_ref[...]) * SCALE
    dv = dot_nn(expo, ga_far)
    for level, out in enumerate(outs):
        out[0] = dk[level * picks : (level + 1) * picks].astype(BF16)
        out[1] = dv[level * picks : (level + 1) * picks].astype(BF16)


def backward_near_kernel(e_ref, ga_ref, delta_ref, q_ref, k_ref, v_ref, dqf_ref, dq_ref, dk_ref, dv_ref, gl_scr, k_scr, qg_scr):
    rows = q_ref.shape[0]

    @pl.when(pl.program_id(0) == 0)
    def _():
        k_scr[:, DH:] = jnp.zeros((rows, DH), BF16)

    k_scr[:, :DH] = k_ref[...]
    qg_scr[:, :DH] = q_ref[...]
    qg_scr[:, DH:] = ga_ref[...]
    for start in range(0, rows, TQ):
        part = pl.ds(start, TQ)
        grad_w = dot_nt(ga_ref[part, :], v_ref[...])
        delta = jnp.concatenate([delta_ref[part, :]] * (rows // LANES), axis=1)
        gl = (e_ref[0, part, :].astype(F32) * (grad_w - delta)).astype(BF16)
        gl_scr[part, :] = gl
        dq_ref[part, :] = ((dot_nn(gl, k_scr[...])[:, :DH] + dqf_ref[part, :]) * SCALE).astype(BF16)
    dk_ref[...] = dot_tn(gl_scr[...], qg_scr[...])[:, :DH] * SCALE
    dv_ref[...] = dot_tn(e_ref[0], qg_scr[...])[:, DH:]


def merge_kernel(levels, off_ref, dk_ref, dv_ref, *rest):
    back = rest[:levels]
    gk_ref, gv_ref, k_scr, v_scr = rest[levels:]
    head = pl.program_id(0)
    picks = dk_ref.shape[0] // RATE
    k_scr[...] = dk_ref[...]
    v_scr[...] = dv_ref[...]
    for level in range(levels):
        spot = pl.ds(off_ref[level, head], picks, stride=RATE)
        k_scr[spot, :] += back[level][0].astype(F32)
        v_scr[spot, :] += back[level][1].astype(F32)
    gk_ref[...] = k_scr[...].astype(BF16)
    gv_ref[...] = v_scr[...].astype(BF16)


def local(queries, key_rows, value_rows, out_grad, norm_gain, offsets, segments, tile_mask):
    rows = queries.shape[0]
    blocks = lax.axis_size("ctx")
    seg_rows = segments.reshape(blocks, rows)
    first, last = seg_rows[:, 0], seg_rows[:, -1]
    index = jnp.arange(blocks, dtype=jnp.int32)
    branch = jnp.int32(0)
    for level in range(1, LEVELS):
        other = [source ^ 2**level for source in range(blocks)]
        low = jnp.maximum(first, jnp.stack([first[i] for i in other]))
        high = jnp.minimum(last, jnp.stack([last[i] for i in other]))
        branch = jnp.where(jnp.any(low <= high), jnp.int32(level), branch)
    own = lax.axis_index("ctx").reshape(1)
    args = (queries, key_rows, value_rows, out_grad, norm_gain, offsets, seg_rows.astype(F32), tile_mask, own)
    return lax.switch(branch, [functools.partial(layer, count + 1) for count in range(LEVELS)], *args)


def layer(levels, queries, key_rows, value_rows, out_grad, norm_gain, offsets, seg_rows, tile_mask, own):
    rows, width = queries.shape
    blocks = seg_rows.shape[0]
    heads = width // DH
    picks = rows // RATE
    total_width = width * lax.axis_size("head")
    queries, key_rows, value_rows, out_grad = [
        pltpu.with_memory_space_constraint(x, pltpu.HBM) for x in (queries, key_rows, value_rows, out_grad)
    ]

    by_head = pl.BlockSpec((rows, DH), lambda h: (0, h))
    seg_spec = pl.BlockSpec((blocks, rows), lambda h: (0, 0))
    pair = pl.BlockSpec((2, picks, DH), lambda h: (0, 0, h))
    stat_rows = pl.BlockSpec((2 * heads, rows), lambda h: (0, 0))
    smem = pl.BlockSpec(memory_space=pltpu.SMEM)
    gain_row = norm_gain.reshape(1, width)
    gain_spec = pl.BlockSpec((1, DH), lambda h: (0, h))

    def call(kernel, name, mib, in_specs, out_specs, out_shape, scratch=(), flops=0, moved=0, expo=0):
        return pl.pallas_call(
            kernel,
            name=name,
            grid=(heads,),
            in_specs=in_specs,
            out_specs=out_specs,
            out_shape=out_shape,
            scratch_shapes=scratch,
            compiler_params=pltpu.CompilerParams(dimension_semantics=("arbitrary",), vmem_limit_bytes=mib << 20),
            cost_estimate=pl.CostEstimate(flops=flops, bytes_accessed=moved, transcendentals=expo),
        )

    def shape(dims, dtype):
        return jax.ShapeDtypeStruct(dims, dtype)

    full = rows * width
    pair_shape = shape((2, picks, width), BF16)
    samples = call(
        sample_kernel,
        "sample",
        5,
        [smem, by_head, by_head],
        [pair] * levels,
        [pair_shape] * levels,
        [pltpu.VMEM((rows, DH), F32)] * 2,
        moved=4 * full,
    )(offsets, key_rows, value_rows)
    recv = [partner(samples[level], "ctx", level) for level in range(levels)]

    square = rows * rows * heads
    expo, acc, stat = call(
        functools.partial(forward_near_kernel, heads),
        "forward_near",
        12,
        [smem, by_head, by_head, by_head, seg_spec],
        [pl.BlockSpec((1, rows, rows), lambda h: (h, 0, 0)), by_head, stat_rows],
        [pltpu.HBM((heads, rows, rows), BF16), shape((rows, width), F32), shape((2 * heads, rows), F32)],
        [pltpu.VMEM((rows, 2 * DH), BF16), pltpu.VMEM((rows, LANES), F32), pltpu.VMEM((rows, LANES), F32)],
        flops=4 * square * DH,
        moved=2 * square + 10 * full,
        expo=square,
    )(own, queries, key_rows, value_rows, seg_rows)

    far_n = levels * picks
    far_spec = pl.BlockSpec((1, far_n, rows), lambda h: (h, 0, 0))
    far_square = rows * far_n * heads
    att, expo_far, rate, sums = call(
        functools.partial(forward_far_kernel, heads, levels),
        "forward_far",
        10,
        [smem, smem, smem, by_head, seg_spec, by_head, stat_rows, by_head, gain_spec]
        + [pair] * levels,
        [by_head, far_spec, stat_rows, pl.BlockSpec((2, rows), lambda h: (0, 0))],
        [shape((rows, width), F32), shape((heads, far_n, rows), BF16), shape((2 * heads, rows), F32), shape((2, rows), F32)],
        [pltpu.VMEM((rows, LANES), F32)] * 2
        + [pltpu.VMEM((levels, rows), F32)]
        + [pltpu.VMEM((rows, LANES), F32)] * levels,
        flops=4 * far_square * DH,
        moved=2 * far_square + 12 * full,
        expo=far_square,
    )(own, offsets, tile_mask, queries, seg_rows, acc, stat, out_grad, gain_row, *recv)
    parts = lax.axis_size("head")
    shifted = [
        lax.ppermute(sums, "head", [(i, (i + step) % parts) for i in range(parts)]) for step in range(1, parts)
    ]
    gathered = [sums] + shifted

    outs = call(
        functools.partial(backward_far_kernel, heads, levels, total_width, parts),
        "backward_far",
        10,
        [pl.BlockSpec((2, rows), lambda h: (0, 0))] * parts
        + [by_head, by_head, gain_spec, stat_rows, by_head, far_spec]
        + [pair] * levels,
        [by_head, by_head, by_head, by_head] + [pair] * levels,
        [shape((rows, width), BF16), shape((rows, width), BF16), shape((rows, width), F32), shape((rows, width), F32)]
        + [pair_shape] * levels,
        [pltpu.VMEM((rows, LANES), F32)] * 2,
        flops=8 * far_square * DH,
        moved=2 * far_square + 16 * full,
    )(*gathered, att, out_grad, gain_row, rate, queries, expo_far, *recv)
    normed, grad_att, delta, dq_far = outs[:4]
    back = [partner(outs[4 + level], "ctx", level) for level in range(levels)]

    grad_queries, dk, dv = call(
        backward_near_kernel,
        "backward_near",
        20,
        [pl.BlockSpec((1, rows, rows), lambda h: (h, 0, 0))] + [by_head] * 6,
        [by_head, by_head, by_head],
        [shape((rows, width), BF16), shape((rows, width), F32), shape((rows, width), F32)],
        [pltpu.VMEM((rows, rows), BF16)] + [pltpu.VMEM((rows, 2 * DH), BF16)] * 2,
        flops=8 * square * DH,
        moved=2 * square + 22 * full,
    )(pltpu.with_memory_space_constraint(expo, pltpu.HBM), grad_att, delta, queries, key_rows, value_rows, dq_far)

    grad_keys, grad_values = call(
        functools.partial(merge_kernel, levels),
        "merge",
        7,
        [smem, by_head, by_head] + [pair] * levels,
        [by_head, by_head],
        [shape((rows, width), BF16)] * 2,
        [pltpu.VMEM((rows, DH), F32)] * 2,
        moved=14 * full,
    )(offsets, dk, dv, *back)
    return (normed, grad_queries, grad_keys, grad_values)


def solution(mesh):
    placed = (
        P("ctx", "head"),
        P("ctx", "head"),
        P("ctx", "head"),
        P("ctx", "head"),
        P("head"),
        P(None, "head"),
        P(),
        P("ctx", None),
    )
    return jax.shard_map(
        local,
        mesh=mesh,
        in_specs=placed,
        out_specs=(P("ctx", "head"), P("ctx", "head"), P("ctx", "head"), P("ctx", "head")),
        check_vma=False,
    )
```

```python
import functools

import jax
import jax.numpy as jnp
from jax import lax
from jax.experimental import pallas as pl
from jax.experimental.pallas import tpu as pltpu
from jax.sharding import PartitionSpec as P

DH = 128
RATE = 8
LEVELS = 3
LANES = 128
BIG = 1e30
EPS = 1e-06
TQ = 256
F32 = jnp.float32
BF16 = jnp.bfloat16
SCALE = DH ** (-0.5)
EXP2_SCALE = SCALE * 1.4426950408889634


def partner(value, axis, bit):
    mask = 2**bit
    pairs = [(source, source ^ mask) for source in range(lax.axis_size(axis))]
    return lax.ppermute(value, axis, pairs)


def dot_nt(a, b):
    return lax.dot_general(a, b, (((1,), (1,)), ((), ())), preferred_element_type=F32)


def dot_nn(a, b):
    return lax.dot_general(a, b, (((1,), (0,)), ((), ())), preferred_element_type=F32)


def dot_tn(a, b):
    return lax.dot_general(a, b, (((0,), (0,)), ((), ())), preferred_element_type=F32)


def lane_of(shape):
    return lax.broadcasted_iota(jnp.int32, shape, 1)


def sample_kernel(off_ref, k_ref, v_ref, *rest):
    outs, (k_scr, v_scr) = rest[:-2], rest[-2:]
    head = pl.program_id(0)
    picks = k_ref.shape[0] // RATE
    k_scr[...] = k_ref[...].astype(F32)
    v_scr[...] = v_ref[...].astype(F32)
    for level, out in enumerate(outs):
        start = off_ref[level, head]
        out[0, 0] = k_scr[pl.ds(start, picks, stride=RATE), :].astype(BF16)
        out[0, 1] = v_scr[pl.ds(start, picks, stride=RATE), :].astype(BF16)


def as_columns(row):
    return jnp.broadcast_to(row, (LANES, row.shape[1])).T


def forward_near_kernel(heads, own_ref, q_ref, k_ref, v_ref, seg_ref, e_ref, acc_ref, stat_ref, va_scr, seg_scr, stat_scr):
    head = pl.program_id(0)
    rows = q_ref.shape[0]
    seg_row = seg_ref[pl.ds(own_ref[0], 1), :]

    @pl.when(head == 0)
    def _():
        va_scr[:, DH:] = jnp.ones((rows, LANES), BF16)
        seg_scr[...] = as_columns(seg_row)

    va_scr[:, :DH] = v_ref[...]
    for start in range(0, rows, TQ):
        part = pl.ds(start, TQ)
        logits = dot_nt(q_ref[part, :], k_ref[...])
        seg_col = jnp.concatenate([seg_scr[part, :]] * (rows // LANES), axis=1)
        logits = jnp.where(seg_col == seg_row, logits, -BIG)
        top = jnp.max(logits, axis=1, keepdims=True)
        expo = jnp.exp2((logits - top) * EXP2_SCALE).astype(BF16)
        e_ref[0, part, :] = expo
        mixed = dot_nn(expo, va_scr[...])
        acc_ref[0, part, :] = mixed[:, :DH]
        lane = lane_of((TQ, LANES))
        kept = jnp.where(lane == head + heads, mixed[:, DH:], stat_scr[part, :])
        stat_scr[part, :] = jnp.where(lane == head, top, kept)

    @pl.when(head == pl.num_programs(0) - 1)
    def _():
        stat_ref[...] = stat_scr[...].T[: 2 * heads, :]


def split_parts(x, count):
    parts = []
    for _ in range(count):
        piece = x.astype(BF16)
        parts.append(piece)
        x = x - piece.astype(F32)
    return parts


def row_sums(x, count):
    ones = jnp.ones((16, x.shape[1]), BF16)
    return sum(dot_nt(ones, piece) for piece in split_parts(x, count))[0:1, :]


def pair_columns(first, second):
    pieces = split_parts(first, 3) + split_parts(second, 3)
    rows = jnp.concatenate(pieces + [jnp.zeros((10, first.shape[1]), BF16)], axis=0)
    source = lax.broadcasted_iota(jnp.int32, (16, 2 * LANES), 0)
    lane = lane_of((16, 2 * LANES))
    spread = jnp.where((source < 3) == (lane < LANES), 1.0, 0.0).astype(BF16)
    wide = dot_tn(rows, spread)
    return wide[:, :LANES], wide[:, LANES:]


def forward_far_kernel(heads, levels, own_ref, off_ref, mask_ref, q_ref, seg_ref, acc_ref, stat_ref, og_ref, gain_ref, *rest):
    recv = rest[:levels]
    att_ref, ef_ref, rate_ref, sums_ref, open_scr = rest[levels : levels + 5]
    seg_scr = rest[levels + 5 :]
    head = pl.program_id(0)
    rows = q_ref.shape[0]
    picks = rows // RATE
    tiles = mask_ref.shape[0]
    tile = rows // tiles
    keys = jnp.concatenate([ref[0, 0] for ref in recv], axis=0)
    values = jnp.concatenate([ref[0, 1] for ref in recv], axis=0)

    @pl.when(head == 0)
    def _():
        sums_ref[...] = jnp.zeros_like(sums_ref)
        own = own_ref[0]
        own_row = seg_ref[pl.ds(own, 1), :]
        for level in range(levels):
            other = jnp.bitwise_xor(own, 2**level)
            seg_scr[level][...] = as_columns(seg_ref[pl.ds(other, 1), :])
            for index in range(tiles):
                span = slice(index * tile, (index + 1) * tile)
                shut = jnp.where(mask_ref[index, level] == 1, 0.0, 1.0)
                open_scr[level : level + 1, span] = own_row[:, span] - 1000.0 * shut

    allowed = []
    for level in range(levels):
        seg_col = seg_scr[level][pl.ds(off_ref[level, head], picks, stride=RATE), :]
        seg_col = jnp.concatenate([seg_col] * (rows // LANES), axis=1)
        allowed.append(seg_col == open_scr[level : level + 1, :])
    logits = dot_nt(keys, q_ref[...])
    logits = jnp.where(jnp.concatenate(allowed, axis=0), logits, -BIG)
    top_far = jnp.max(logits, axis=0, keepdims=True)
    expo = jnp.exp2((logits - top_far) * EXP2_SCALE).astype(BF16)
    ef_ref[0] = expo
    mixed = dot_tn(expo, values)
    sum_far = dot_nn(jnp.ones((16, expo.shape[0]), BF16), expo)[0:1, :]
    top_near = stat_ref[pl.ds(head, 1), :]
    sum_near = stat_ref[pl.ds(head + heads, 1), :]
    top = jnp.maximum(top_near, top_far)
    a_near = jnp.exp2((top_near - top) * EXP2_SCALE)
    a_far = jnp.exp2((top_far - top) * EXP2_SCALE)
    inv = 1.0 / (a_near * sum_near + a_far * sum_far)
    r_near = a_near * inv
    r_far = a_far * inv
    rate_ref[pl.ds(head, 1), :] = r_near
    rate_ref[pl.ds(head + heads, 1), :] = r_far
    near_col, far_col = pair_columns(r_near, r_far)
    att = near_col * acc_ref[0] + far_col * mixed
    att_ref[0] = att
    scaled = og_ref[...].astype(F32) * gain_ref[...]
    sums_ref[0:1, :] += row_sums(att * att, 2)
    sums_ref[1:2, :] += row_sums(scaled * att, 2)


def backward_far_kernel(heads, levels, width, parts, *refs):
    gathered = refs[:parts]
    att_ref, og_ref, gain_ref, rate_ref, q_ref, ef_ref = refs[parts : parts + 6]
    rest = refs[parts + 6 :]
    recv = rest[:levels]
    normed_ref, ga_ref, delta_ref, dq_ref = rest[levels : levels + 4]
    outs = rest[levels + 4 : levels + 4 + levels]
    inv_scr, cc_scr = rest[levels + 4 + levels :]
    head = pl.program_id(0)
    rows = q_ref.shape[0]
    picks = rows // RATE

    @pl.when(head == 0)
    def _():
        sums = functools.reduce(jnp.add, [ref[...] for ref in gathered])
        inv_row = lax.rsqrt(sums[0:1, :] / width + EPS)
        inv_scr[...] = as_columns(inv_row)
        cc_scr[...] = as_columns(inv_row * inv_row * (sums[1:2, :] / width))

    keys = jnp.concatenate([ref[0, 0] for ref in recv], axis=0)
    values = jnp.concatenate([ref[0, 1] for ref in recv], axis=0)
    gain = gain_ref[...]
    att = att_ref[0]
    inv = inv_scr[...]
    normed_ref[...] = (att * inv * gain).astype(BF16)
    scaled = og_ref[...].astype(F32) * gain
    grad_att = inv * (scaled - att * cc_scr[...])
    ga_near = (grad_att * as_columns(rate_ref[pl.ds(head, 1), :])).astype(BF16)
    ga_far = (grad_att * as_columns(rate_ref[pl.ds(head + heads, 1), :])).astype(BF16)
    ga_ref[0] = ga_near
    delta_near = jnp.sum(ga_near.astype(F32) * att, axis=1, keepdims=True)
    delta_ref[0] = jnp.broadcast_to(delta_near, (rows, LANES))
    delta_far = jnp.sum((ga_far.astype(F32) * att).T, axis=0, keepdims=True)
    grad_w = dot_nt(values, ga_far)
    expo = ef_ref[0]
    gl = (expo.astype(F32) * (grad_w - delta_far)).astype(BF16)
    dq_ref[0] = dot_tn(gl, keys)
    dk = dot_nn(gl, q_ref[...]) * SCALE
    dv = dot_nn(expo, ga_far)
    for level, out in enumerate(outs):
        out[0, 0] = dk[level * picks : (level + 1) * picks].astype(BF16)
        out[0, 1] = dv[level * picks : (level + 1) * picks].astype(BF16)


def backward_near_kernel(e_ref, ga_ref, delta_ref, q_ref, k_ref, v_ref, dqf_ref, dq_ref, dk_ref, dv_ref, gl_scr, k_scr, qg_scr):
    rows = q_ref.shape[0]

    @pl.when(pl.program_id(0) == 0)
    def _():
        k_scr[:, DH:] = jnp.zeros((rows, DH), BF16)

    k_scr[:, :DH] = k_ref[...]
    qg_scr[:, :DH] = q_ref[...]
    qg_scr[:, DH:] = ga_ref[0]
    for start in range(0, rows, TQ):
        part = pl.ds(start, TQ)
        grad_w = dot_nt(ga_ref[0, part, :], v_ref[...])
        delta = jnp.concatenate([delta_ref[0, part, :]] * (rows // LANES), axis=1)
        gl = (e_ref[0, part, :].astype(F32) * (grad_w - delta)).astype(BF16)
        gl_scr[part, :] = gl
        dq_ref[part, :] = ((dot_nn(gl, k_scr[...])[:, :DH] + dqf_ref[0, part, :]) * SCALE).astype(BF16)
    dk_ref[0] = dot_tn(gl_scr[...], qg_scr[...])[:, :DH] * SCALE
    dv_ref[0] = dot_tn(e_ref[0], qg_scr[...])[:, DH:]


def merge_kernel(levels, off_ref, dk_ref, dv_ref, *rest):
    back = rest[:levels]
    gk_ref, gv_ref, k_scr, v_scr = rest[levels:]
    head = pl.program_id(0)
    picks = dk_ref.shape[1] // RATE
    k_scr[...] = dk_ref[0]
    v_scr[...] = dv_ref[0]
    for level in range(levels):
        spot = pl.ds(off_ref[level, head], picks, stride=RATE)
        k_scr[spot, :] += back[level][0, 0].astype(F32)
        v_scr[spot, :] += back[level][0, 1].astype(F32)
    gk_ref[...] = k_scr[...].astype(BF16)
    gv_ref[...] = v_scr[...].astype(BF16)


def local(queries, key_rows, value_rows, out_grad, norm_gain, offsets, segments, tile_mask):
    rows = queries.shape[0]
    blocks = lax.axis_size("ctx")
    seg_rows = segments.reshape(blocks, rows)
    first, last = seg_rows[:, 0], seg_rows[:, -1]
    branch = jnp.int32(0)
    for level in range(1, LEVELS):
        low, high = first.reshape(-1, 2, 2**level), last.reshape(-1, 2, 2**level)
        meet = jnp.max(low, axis=1) <= jnp.min(high, axis=1)
        branch = jnp.where(jnp.any(meet), jnp.int32(level), branch)
    own = lax.axis_index("ctx").reshape(1)
    args = (queries, key_rows, value_rows, out_grad, norm_gain, offsets, seg_rows.astype(F32), tile_mask, own)
    return lax.switch(branch, [functools.partial(layer, count + 1) for count in range(LEVELS)], *args)


def layer(levels, queries, key_rows, value_rows, out_grad, norm_gain, offsets, seg_rows, tile_mask, own):
    rows, width = queries.shape
    blocks = seg_rows.shape[0]
    heads = width // DH
    picks = rows // RATE
    total_width = width * lax.axis_size("head")
    queries, key_rows, value_rows, out_grad = [
        pltpu.with_memory_space_constraint(x, pltpu.HBM) for x in (queries, key_rows, value_rows, out_grad)
    ]

    by_head = pl.BlockSpec((rows, DH), lambda h: (0, h))
    seg_spec = pl.BlockSpec((blocks, rows), lambda h: (0, 0))
    pair = pl.BlockSpec((1, 2, picks, DH), lambda h: (h, 0, 0, 0))
    major = pl.BlockSpec((1, rows, DH), lambda h: (h, 0, 0))
    major_f = jax.ShapeDtypeStruct((heads, rows, DH), F32)
    major_b = jax.ShapeDtypeStruct((heads, rows, DH), BF16)
    stat_rows = pl.BlockSpec((2 * heads, rows), lambda h: (0, 0))
    smem = pl.BlockSpec(memory_space=pltpu.SMEM)
    gain_row = norm_gain.reshape(1, width)
    gain_spec = pl.BlockSpec((1, DH), lambda h: (0, h))

    def call(kernel, name, mib, in_specs, out_specs, out_shape, scratch=(), flops=0, moved=0, expo=0):
        return pl.pallas_call(
            kernel,
            name=name,
            grid=(heads,),
            in_specs=in_specs,
            out_specs=out_specs,
            out_shape=out_shape,
            scratch_shapes=scratch,
            compiler_params=pltpu.CompilerParams(dimension_semantics=("arbitrary",), vmem_limit_bytes=mib << 20),
            cost_estimate=pl.CostEstimate(flops=flops, bytes_accessed=moved, transcendentals=expo),
        )

    def shape(dims, dtype):
        return jax.ShapeDtypeStruct(dims, dtype)

    full = rows * width
    pair_shape = shape((heads, 2, picks, DH), BF16)
    samples = call(
        sample_kernel,
        "sample",
        5,
        [smem, by_head, by_head],
        [pair] * levels,
        [pair_shape] * levels,
        [pltpu.VMEM((rows, DH), F32)] * 2,
        moved=4 * full,
    )(offsets, key_rows, value_rows)
    recv = [partner(samples[level], "ctx", level) for level in range(levels)]

    square = rows * rows * heads
    expo, acc, stat = call(
        functools.partial(forward_near_kernel, heads),
        "forward_near",
        12,
        [smem, by_head, by_head, by_head, seg_spec],
        [pl.BlockSpec((1, rows, rows), lambda h: (h, 0, 0)), major, stat_rows],
        [pltpu.HBM((heads, rows, rows), BF16), major_f, shape((2 * heads, rows), F32)],
        [pltpu.VMEM((rows, 2 * DH), BF16), pltpu.VMEM((rows, LANES), F32), pltpu.VMEM((rows, LANES), F32)],
        flops=4 * square * DH,
        moved=2 * square + 10 * full,
        expo=square,
    )(own, queries, key_rows, value_rows, seg_rows)

    far_n = levels * picks
    far_spec = pl.BlockSpec((1, far_n, rows), lambda h: (h, 0, 0))
    far_square = rows * far_n * heads
    att, expo_far, rate, sums = call(
        functools.partial(forward_far_kernel, heads, levels),
        "forward_far",
        10,
        [smem, smem, smem, by_head, seg_spec, major, stat_rows, by_head, gain_spec]
        + [pair] * levels,
        [major, far_spec, stat_rows, pl.BlockSpec((2, rows), lambda h: (0, 0))],
        [major_f, shape((heads, far_n, rows), BF16), shape((2 * heads, rows), F32), shape((2, rows), F32)],
        [pltpu.VMEM((levels, rows), F32)]
        + [pltpu.VMEM((rows, LANES), F32)] * levels,
        flops=4 * far_square * DH,
        moved=2 * far_square + 12 * full,
        expo=far_square,
    )(own, offsets, tile_mask, queries, seg_rows, acc, stat, out_grad, gain_row, *recv)
    parts = lax.axis_size("head")
    shifted = [
        lax.ppermute(sums, "head", [(i, (i + step) % parts) for i in range(parts)]) for step in range(1, parts)
    ]
    gathered = [sums] + shifted

    outs = call(
        functools.partial(backward_far_kernel, heads, levels, total_width, parts),
        "backward_far",
        10,
        [pl.BlockSpec((2, rows), lambda h: (0, 0))] * parts
        + [major, by_head, gain_spec, stat_rows, by_head, far_spec]
        + [pair] * levels,
        [by_head, major, major, major] + [pair] * levels,
        [shape((rows, width), BF16), major_b, major_f, major_f]
        + [pair_shape] * levels,
        [pltpu.VMEM((rows, LANES), F32)] * 2,
        flops=8 * far_square * DH,
        moved=2 * far_square + 16 * full,
    )(*gathered, att, out_grad, gain_row, rate, queries, expo_far, *recv)
    normed, grad_att, delta, dq_far = outs[:4]
    back = [partner(outs[4 + level], "ctx", level) for level in range(levels)]

    grad_queries, dk, dv = call(
        backward_near_kernel,
        "backward_near",
        20,
        [pl.BlockSpec((1, rows, rows), lambda h: (h, 0, 0)), major, major, by_head, by_head, by_head, major],
        [by_head, major, major],
        [shape((rows, width), BF16), major_f, major_f],
        [pltpu.VMEM((rows, rows), BF16)] + [pltpu.VMEM((rows, 2 * DH), BF16)] * 2,
        flops=8 * square * DH,
        moved=2 * square + 22 * full,
    )(pltpu.with_memory_space_constraint(expo, pltpu.HBM), grad_att, delta, queries, key_rows, value_rows, dq_far)

    grad_keys, grad_values = call(
        functools.partial(merge_kernel, levels),
        "merge",
        7,
        [smem, major, major] + [pair] * levels,
        [by_head, by_head],
        [shape((rows, width), BF16)] * 2,
        [pltpu.VMEM((rows, DH), F32)] * 2,
        moved=14 * full,
    )(offsets, dk, dv, *back)
    return (normed, grad_queries, grad_keys, grad_values)


def solution(mesh):
    placed = (
        P("ctx", "head"),
        P("ctx", "head"),
        P("ctx", "head"),
        P("ctx", "head"),
        P("head"),
        P(None, "head"),
        P(),
        P("ctx", None),
    )
    return jax.shard_map(
        local,
        mesh=mesh,
        in_specs=placed,
        out_specs=(P("ctx", "head"), P("ctx", "head"), P("ctx", "head"), P("ctx", "head")),
        check_vma=False,
    )
```

```python
import functools

import jax
import jax.numpy as jnp
from jax import lax
from jax.experimental import pallas as pl
from jax.experimental.pallas import tpu as pltpu
from jax.sharding import PartitionSpec as P

DH = 128
RATE = 8
LEVELS = 3
LANES = 128
BIG = 1e30
EPS = 1e-06
TQ = 256
GROUP = 2
SUM_LIMIT = 2.0**60
F32 = jnp.float32
BF16 = jnp.bfloat16
SCALE = DH ** (-0.5)
EXP2_SCALE = SCALE * 1.4426950408889634


def partner(value, axis, bit):
    mask = 2**bit
    pairs = [(source, source ^ mask) for source in range(lax.axis_size(axis))]
    return lax.ppermute(value, axis, pairs)


def dot_nt(a, b):
    return lax.dot_general(a, b, (((1,), (1,)), ((), ())), preferred_element_type=F32)


def dot_nn(a, b):
    return lax.dot_general(a, b, (((1,), (0,)), ((), ())), preferred_element_type=F32)


def dot_tn(a, b):
    return lax.dot_general(a, b, (((0,), (0,)), ((), ())), preferred_element_type=F32)


def lane_of(shape):
    return lax.broadcasted_iota(jnp.int32, shape, 1)


def sample_kernel(off_ref, k_ref, v_ref, *rest):
    outs, (k_scr, v_scr) = rest[:-2], rest[-2:]
    head = pl.program_id(0)
    picks = k_ref.shape[0] // RATE
    k_scr[...] = k_ref[...].astype(F32)
    v_scr[...] = v_ref[...].astype(F32)
    for level, out in enumerate(outs):
        start = off_ref[level, head]
        out[0, 0] = k_scr[pl.ds(start, picks, stride=RATE), :].astype(BF16)
        out[0, 1] = v_scr[pl.ds(start, picks, stride=RATE), :].astype(BF16)


def as_columns(row):
    return jnp.broadcast_to(row, (LANES, row.shape[1])).T


def forward_near_kernel(
    heads, own_ref, q_ref, k_ref, v_ref, seg_ref, e_ref, acc_ref, stat_ref, qa_scr, ka_scr, va_scr, stat_scr
):
    head = pl.program_id(0)
    rows = q_ref.shape[0]

    @pl.when(head == 0)
    def _():
        same = as_columns(seg_ref[pl.ds(own_ref[0], 1), :]) == lane_of((rows, LANES)).astype(F32)
        qa_scr[:, DH:] = jnp.where(same, 1.0, 0.0).astype(BF16)
        ka_scr[:, DH:] = jnp.where(same, 0.0, -BIG).astype(BF16)
        va_scr[:, DH:] = jnp.ones((rows, LANES), BF16)

    qa_scr[:, :DH] = q_ref[...]
    ka_scr[:, :DH] = k_ref[...]
    va_scr[:, :DH] = v_ref[...]

    def weigh(parts, pick):
        every = [dot_nt(qa_scr[part, :], ka_scr[...]) for part in parts]
        return every, [pick(part, logits) for part, logits in zip(parts, every)]

    def expose(parts, every, shifts):
        for part, logits, shift in zip(parts, every, shifts):
            e_ref[0, part, :] = jnp.exp2((logits - shift) * EXP2_SCALE).astype(BF16)

    def mix(parts, shifts):
        lane = lane_of((TQ, LANES))
        sums = []
        for part, shift in zip(parts, shifts):
            mixed = dot_nn(e_ref[0, part, :], va_scr[...])
            acc_ref[0, part, :] = mixed[:, :DH]
            kept = jnp.where(lane == head + heads, mixed[:, DH:], stat_scr[part, :])
            stat_scr[part, :] = jnp.where(lane == head, shift, kept)
            sums.append(mixed[:, DH:])
        return sums

    def own_logit(part, logits):
        return jnp.sum(q_ref[part, :].astype(F32) * k_ref[part, :].astype(F32), axis=1, keepdims=True)

    def top_logit(part, logits):
        return jnp.max(logits, axis=1, keepdims=True)

    sums, waiting = [], None
    for start in range(0, rows, GROUP * TQ):
        parts = [pl.ds(start + index * TQ, TQ) for index in range(GROUP)]
        every, shifts = weigh(parts, own_logit)
        if waiting is not None:
            sums += mix(*waiting)
        expose(parts, every, shifts)
        waiting = (parts, shifts)
    sums += mix(*waiting)
    safe = jnp.max(functools.reduce(jnp.maximum, sums)) <= SUM_LIMIT

    @pl.when(jnp.logical_not(safe))
    def _():
        @pl.loop(0, rows // TQ)
        def _(index):
            parts = [pl.ds(pl.multiple_of(index * TQ, TQ), TQ)]
            every, shifts = weigh(parts, top_logit)
            expose(parts, every, shifts)
            mix(parts, shifts)

    @pl.when(head == pl.num_programs(0) - 1)
    def _():
        stat_ref[...] = stat_scr[...].T[: 2 * heads, :]


def split_parts(x, count):
    parts = []
    for _ in range(count):
        piece = x.astype(BF16)
        parts.append(piece)
        x = x - piece.astype(F32)
    return parts


def row_sums(x, count):
    ones = jnp.ones((16, x.shape[1]), BF16)
    return sum(dot_nt(ones, piece) for piece in split_parts(x, count))[0:1, :]


def pair_columns(first, second):
    pieces = split_parts(first, 3) + split_parts(second, 3)
    rows = jnp.concatenate(pieces + [jnp.zeros((10, first.shape[1]), BF16)], axis=0)
    source = lax.broadcasted_iota(jnp.int32, (16, 2 * LANES), 0)
    lane = lane_of((16, 2 * LANES))
    spread = jnp.where((source < 3) == (lane < LANES), 1.0, 0.0).astype(BF16)
    wide = dot_tn(rows, spread)
    return wide[:, :LANES], wide[:, LANES:]


def forward_far_kernel(heads, levels, own_ref, off_ref, mask_ref, q_ref, seg_ref, acc_ref, stat_ref, og_ref, gain_ref, *rest):
    recv = rest[:levels]
    att_ref, ef_ref, rate_ref, sums_ref, open_scr = rest[levels : levels + 5]
    seg_scr = rest[levels + 5 :]
    head = pl.program_id(0)
    rows = q_ref.shape[0]
    picks = rows // RATE
    tiles = mask_ref.shape[0]
    tile = rows // tiles
    keys = jnp.concatenate([ref[0, 0] for ref in recv], axis=0)
    values = jnp.concatenate([ref[0, 1] for ref in recv], axis=0)

    @pl.when(head == 0)
    def _():
        sums_ref[...] = jnp.zeros_like(sums_ref)
        own = own_ref[0]
        own_row = seg_ref[pl.ds(own, 1), :]
        for level in range(levels):
            other = jnp.bitwise_xor(own, 2**level)
            seg_scr[level][...] = as_columns(seg_ref[pl.ds(other, 1), :])
            for index in range(tiles):
                span = slice(index * tile, (index + 1) * tile)
                shut = jnp.where(mask_ref[index, level] == 1, 0.0, 1.0)
                open_scr[level : level + 1, span] = own_row[:, span] - 1000.0 * shut

    allowed = []
    for level in range(levels):
        seg_col = seg_scr[level][pl.ds(off_ref[level, head], picks, stride=RATE), :]
        seg_col = jnp.concatenate([seg_col] * (rows // LANES), axis=1)
        allowed.append(seg_col == open_scr[level : level + 1, :])
    logits = dot_nt(keys, q_ref[...])
    logits = jnp.where(jnp.concatenate(allowed, axis=0), logits, -BIG)
    top_far = jnp.max(logits, axis=0, keepdims=True)
    expo = jnp.exp2((logits - top_far) * EXP2_SCALE).astype(BF16)
    ef_ref[0] = expo
    mixed = dot_tn(expo, values)
    sum_far = dot_nn(jnp.ones((16, expo.shape[0]), BF16), expo)[0:1, :]
    top_near = stat_ref[pl.ds(head, 1), :]
    sum_near = stat_ref[pl.ds(head + heads, 1), :]
    top = jnp.maximum(top_near, top_far)
    a_near = jnp.exp2((top_near - top) * EXP2_SCALE)
    a_far = jnp.exp2((top_far - top) * EXP2_SCALE)
    inv = 1.0 / (a_near * sum_near + a_far * sum_far)
    r_near = a_near * inv
    r_far = a_far * inv
    rate_ref[pl.ds(head, 1), :] = r_near
    rate_ref[pl.ds(head + heads, 1), :] = r_far
    near_col, far_col = pair_columns(r_near, r_far)
    att = near_col * acc_ref[0] + far_col * mixed
    att_ref[0] = att
    scaled = og_ref[...].astype(F32) * gain_ref[...]
    sums_ref[0:1, :] += row_sums(att * att, 2)
    sums_ref[1:2, :] += row_sums(scaled * att, 2)


def backward_far_kernel(heads, levels, width, parts, *refs):
    gathered = refs[:parts]
    att_ref, og_ref, gain_ref, rate_ref, q_ref, ef_ref = refs[parts : parts + 6]
    rest = refs[parts + 6 :]
    recv = rest[:levels]
    normed_ref, ga_ref, delta_ref, dq_ref = rest[levels : levels + 4]
    outs = rest[levels + 4 : levels + 4 + levels]
    inv_scr, cc_scr = rest[levels + 4 + levels :]
    head = pl.program_id(0)
    rows = q_ref.shape[0]
    picks = rows // RATE

    @pl.when(head == 0)
    def _():
        sums = functools.reduce(jnp.add, [ref[...] for ref in gathered])
        inv_row = lax.rsqrt(sums[0:1, :] / width + EPS)
        inv_scr[...] = as_columns(inv_row)
        cc_scr[...] = as_columns(inv_row * inv_row * (sums[1:2, :] / width))

    keys = jnp.concatenate([ref[0, 0] for ref in recv], axis=0)
    values = jnp.concatenate([ref[0, 1] for ref in recv], axis=0)
    gain = gain_ref[...]
    att = att_ref[0]
    inv = inv_scr[...]
    normed_ref[...] = (att * inv * gain).astype(BF16)
    scaled = og_ref[...].astype(F32) * gain
    grad_att = inv * (scaled - att * cc_scr[...])
    ga_near = (grad_att * as_columns(rate_ref[pl.ds(head, 1), :])).astype(BF16)
    ga_far = (grad_att * as_columns(rate_ref[pl.ds(head + heads, 1), :])).astype(BF16)
    ga_ref[0] = ga_near
    delta_near = jnp.sum(ga_near.astype(F32) * att, axis=1, keepdims=True)
    delta_ref[0] = jnp.broadcast_to(delta_near, (rows, LANES))
    delta_far = jnp.sum((ga_far.astype(F32) * att).T, axis=0, keepdims=True)
    grad_w = dot_nt(values, ga_far)
    expo = ef_ref[0]
    gl = (expo.astype(F32) * (grad_w - delta_far)).astype(BF16)
    dq_ref[0] = dot_tn(gl, keys)
    dk = dot_nn(gl, q_ref[...]) * SCALE
    dv = dot_nn(expo, ga_far)
    for level, out in enumerate(outs):
        out[0, 0] = dk[level * picks : (level + 1) * picks].astype(BF16)
        out[0, 1] = dv[level * picks : (level + 1) * picks].astype(BF16)


def fold(wide, far):
    return ((wide[:, :DH] + wide[:, DH:] + far) * SCALE).astype(BF16)


def backward_near_kernel(e_ref, ga_ref, delta_ref, q_ref, k_ref, v_ref, dqf_ref, dq_ref, dk_ref, dv_ref, gl_scr, k_scr, qg_scr):
    rows = q_ref.shape[0]

    @pl.when(pl.program_id(0) == 0)
    def _():
        k_scr[:, DH:] = jnp.zeros((rows, DH), BF16)

    k_scr[:, :DH] = k_ref[...]
    qg_scr[:, :DH] = q_ref[...]
    qg_scr[:, DH:] = ga_ref[0]
    waiting = []
    for start in range(0, rows, TQ):
        part = pl.ds(start, TQ)
        grad_w = dot_nt(ga_ref[0, part, :], v_ref[...])
        for done in waiting:
            dq_ref[done, :] = fold(dot_nn(gl_scr[done, :], k_scr[...]), dqf_ref[0, done, :])
        delta = jnp.concatenate([delta_ref[0, part, :]] * (rows // LANES), axis=1)
        gl_scr[part, :] = (e_ref[0, part, :].astype(F32) * (grad_w - delta)).astype(BF16)
        waiting = [part]
    for done in waiting:
        dq_ref[done, :] = fold(dot_nn(gl_scr[done, :], k_scr[...]), dqf_ref[0, done, :])
    dk_ref[0] = dot_nn(q_ref[...].T, gl_scr[...]).T * SCALE
    dv_ref[0] = dot_nn(ga_ref[0].T, e_ref[0]).T


def merge_kernel(levels, off_ref, dk_ref, dv_ref, *rest):
    back = rest[:levels]
    gk_ref, gv_ref, k_scr, v_scr = rest[levels:]
    head = pl.program_id(0)
    picks = dk_ref.shape[1] // RATE
    k_scr[...] = dk_ref[0]
    v_scr[...] = dv_ref[0]
    for level in range(levels):
        spot = pl.ds(off_ref[level, head], picks, stride=RATE)
        k_scr[spot, :] += back[level][0, 0].astype(F32)
        v_scr[spot, :] += back[level][0, 1].astype(F32)
    gk_ref[...] = k_scr[...].astype(BF16)
    gv_ref[...] = v_scr[...].astype(BF16)


def local(queries, key_rows, value_rows, out_grad, norm_gain, offsets, segments, tile_mask):
    rows = queries.shape[0]
    blocks = lax.axis_size("ctx")
    seg_rows = segments.reshape(blocks, rows)
    first, last = seg_rows[:, 0], seg_rows[:, -1]
    branch = jnp.int32(0)
    for level in range(1, LEVELS):
        low, high = first.reshape(-1, 2, 2**level), last.reshape(-1, 2, 2**level)
        meet = jnp.max(low, axis=1) <= jnp.min(high, axis=1)
        branch = jnp.where(jnp.any(meet), jnp.int32(level), branch)
    own = lax.axis_index("ctx").reshape(1)
    args = (queries, key_rows, value_rows, out_grad, norm_gain, offsets, seg_rows.astype(F32), tile_mask, own)
    return lax.switch(branch, [functools.partial(layer, count + 1) for count in range(LEVELS)], *args)


def layer(levels, queries, key_rows, value_rows, out_grad, norm_gain, offsets, seg_rows, tile_mask, own):
    rows, width = queries.shape
    blocks = seg_rows.shape[0]
    heads = width // DH
    picks = rows // RATE
    total_width = width * lax.axis_size("head")
    queries, key_rows, value_rows, out_grad = [
        pltpu.with_memory_space_constraint(x, pltpu.HBM) for x in (queries, key_rows, value_rows, out_grad)
    ]

    by_head = pl.BlockSpec((rows, DH), lambda h: (0, h))
    seg_spec = pl.BlockSpec((blocks, rows), lambda h: (0, 0))
    pair = pl.BlockSpec((1, 2, picks, DH), lambda h: (h, 0, 0, 0))
    major = pl.BlockSpec((1, rows, DH), lambda h: (h, 0, 0))
    major_f = jax.ShapeDtypeStruct((heads, rows, DH), F32)
    major_b = jax.ShapeDtypeStruct((heads, rows, DH), BF16)
    stat_rows = pl.BlockSpec((2 * heads, rows), lambda h: (0, 0))
    smem = pl.BlockSpec(memory_space=pltpu.SMEM)
    gain_row = norm_gain.reshape(1, width)
    gain_spec = pl.BlockSpec((1, DH), lambda h: (0, h))

    def call(kernel, name, mib, in_specs, out_specs, out_shape, scratch=(), flops=0, moved=0, expo=0):
        return pl.pallas_call(
            kernel,
            name=name,
            grid=(heads,),
            in_specs=in_specs,
            out_specs=out_specs,
            out_shape=out_shape,
            scratch_shapes=scratch,
            compiler_params=pltpu.CompilerParams(dimension_semantics=("arbitrary",), vmem_limit_bytes=mib << 20),
            cost_estimate=pl.CostEstimate(flops=flops, bytes_accessed=moved, transcendentals=expo),
        )

    def shape(dims, dtype):
        return jax.ShapeDtypeStruct(dims, dtype)

    full = rows * width
    pair_shape = shape((heads, 2, picks, DH), BF16)
    samples = call(
        sample_kernel,
        "sample",
        5,
        [smem, by_head, by_head],
        [pair] * levels,
        [pair_shape] * levels,
        [pltpu.VMEM((rows, DH), F32)] * 2,
        moved=4 * full,
    )(offsets, key_rows, value_rows)
    recv = [partner(samples[level], "ctx", level) for level in range(levels)]

    square = rows * rows * heads
    expo, acc, stat = call(
        functools.partial(forward_near_kernel, heads),
        "forward_near",
        12,
        [smem, by_head, by_head, by_head, seg_spec],
        [pl.BlockSpec((1, rows, rows), lambda h: (h, 0, 0)), major, stat_rows],
        [pltpu.HBM((heads, rows, rows), BF16), major_f, shape((2 * heads, rows), F32)],
        [pltpu.VMEM((rows, 2 * DH), BF16)] * 3 + [pltpu.VMEM((rows, LANES), F32)],
        flops=4 * square * DH,
        moved=2 * square + 10 * full,
        expo=square,
    )(own, queries, key_rows, value_rows, seg_rows)

    far_n = levels * picks
    far_spec = pl.BlockSpec((1, far_n, rows), lambda h: (h, 0, 0))
    far_square = rows * far_n * heads
    att, expo_far, rate, sums = call(
        functools.partial(forward_far_kernel, heads, levels),
        "forward_far",
        10,
        [smem, smem, smem, by_head, seg_spec, major, stat_rows, by_head, gain_spec]
        + [pair] * levels,
        [major, far_spec, stat_rows, pl.BlockSpec((2, rows), lambda h: (0, 0))],
        [major_f, shape((heads, far_n, rows), BF16), shape((2 * heads, rows), F32), shape((2, rows), F32)],
        [pltpu.VMEM((levels, rows), F32)]
        + [pltpu.VMEM((rows, LANES), F32)] * levels,
        flops=4 * far_square * DH,
        moved=2 * far_square + 12 * full,
        expo=far_square,
    )(own, offsets, tile_mask, queries, seg_rows, acc, stat, out_grad, gain_row, *recv)
    parts = lax.axis_size("head")
    shifted = [
        lax.ppermute(sums, "head", [(i, (i + step) % parts) for i in range(parts)]) for step in range(1, parts)
    ]
    gathered = [sums] + shifted

    outs = call(
        functools.partial(backward_far_kernel, heads, levels, total_width, parts),
        "backward_far",
        10,
        [pl.BlockSpec((2, rows), lambda h: (0, 0))] * parts
        + [major, by_head, gain_spec, stat_rows, by_head, far_spec]
        + [pair] * levels,
        [by_head, major, major, major] + [pair] * levels,
        [shape((rows, width), BF16), major_b, major_f, major_f]
        + [pair_shape] * levels,
        [pltpu.VMEM((rows, LANES), F32)] * 2,
        flops=8 * far_square * DH,
        moved=2 * far_square + 16 * full,
    )(*gathered, att, out_grad, gain_row, rate, queries, expo_far, *recv)
    normed, grad_att, delta, dq_far = outs[:4]
    back = [partner(outs[4 + level], "ctx", level) for level in range(levels)]

    grad_queries, dk, dv = call(
        backward_near_kernel,
        "backward_near",
        20,
        [pl.BlockSpec((1, rows, rows), lambda h: (h, 0, 0)), major, major, by_head, by_head, by_head, major],
        [by_head, major, major],
        [shape((rows, width), BF16), major_f, major_f],
        [pltpu.VMEM((rows, rows), BF16)] + [pltpu.VMEM((rows, 2 * DH), BF16)] * 2,
        flops=8 * square * DH,
        moved=2 * square + 22 * full,
    )(pltpu.with_memory_space_constraint(expo, pltpu.HBM), grad_att, delta, queries, key_rows, value_rows, dq_far)

    grad_keys, grad_values = call(
        functools.partial(merge_kernel, levels),
        "merge",
        7,
        [smem, major, major] + [pair] * levels,
        [by_head, by_head],
        [shape((rows, width), BF16)] * 2,
        [pltpu.VMEM((rows, DH), F32)] * 2,
        moved=14 * full,
    )(offsets, dk, dv, *back)
    return (normed, grad_queries, grad_keys, grad_values)


def solution(mesh):
    placed = (
        P("ctx", "head"),
        P("ctx", "head"),
        P("ctx", "head"),
        P("ctx", "head"),
        P("head"),
        P(None, "head"),
        P(),
        P("ctx", None),
    )
    return jax.shard_map(
        local,
        mesh=mesh,
        in_specs=placed,
        out_specs=(P("ctx", "head"), P("ctx", "head"), P("ctx", "head"), P("ctx", "head")),
        check_vma=False,
    )
```

```python
import functools

import jax
import jax.numpy as jnp
from jax import lax
from jax.experimental import pallas as pl
from jax.experimental.pallas import tpu as pltpu
from jax.sharding import PartitionSpec as P

DH = 128
RATE = 8
LEVELS = 3
LANES = 128
BIG = 1e30
EPS = 1e-06
TQ = 256
GROUP = 2
SUM_LIMIT = 2.0**60
F32 = jnp.float32
BF16 = jnp.bfloat16
SCALE = DH ** (-0.5)
EXP2_SCALE = SCALE * 1.4426950408889634


def partner(value, axis, bit):
    mask = 2**bit
    pairs = [(source, source ^ mask) for source in range(lax.axis_size(axis))]
    return lax.ppermute(value, axis, pairs)


def dot_nt(a, b):
    return lax.dot_general(a, b, (((1,), (1,)), ((), ())), preferred_element_type=F32)


def dot_nn(a, b):
    return lax.dot_general(a, b, (((1,), (0,)), ((), ())), preferred_element_type=F32)


def dot_tn(a, b):
    return lax.dot_general(a, b, (((0,), (0,)), ((), ())), preferred_element_type=F32)


def lane_of(shape):
    return lax.broadcasted_iota(jnp.int32, shape, 1)


def lanes(ref, sub):
    return ref.at[:, pl.ds(sub * DH, DH)]


def lead(ref, sub):
    return ref.at[pl.ds(sub, 1)]


def sample_kernel(per, blocks, rows, seg_ref, off_ref, k_ref, v_ref, branch_ref, *rest):
    outs, (k_scr, v_scr) = rest[:-2], rest[-2:]
    step = pl.program_id(0)
    picks = rows // RATE

    @pl.when(step == 0)
    def _():
        first = [seg_ref[block * rows] for block in range(blocks)]
        last = [seg_ref[block * rows + rows - 1] for block in range(blocks)]
        branch = jnp.int32(0)
        for level in range(1, LEVELS):
            meet = jnp.int32(0)
            for block in range(blocks):
                other = block ^ 2**level
                if block < other:
                    near = jnp.maximum(first[block], first[other]) <= jnp.minimum(last[block], last[other])
                    meet = jnp.where(near, jnp.int32(1), meet)
            branch = jnp.where(meet == 1, jnp.int32(level), branch)
        branch_ref[0] = branch

    for sub in range(per):
        k_scr[...] = lanes(k_ref, sub)[...].astype(F32)
        v_scr[...] = lanes(v_ref, sub)[...].astype(F32)
        for level, out in enumerate(outs):
            start = off_ref[level, step * per + sub]
            out[sub, 0] = k_scr[pl.ds(start, picks, stride=RATE), :].astype(BF16)
            out[sub, 1] = v_scr[pl.ds(start, picks, stride=RATE), :].astype(BF16)


def as_columns(row):
    return jnp.broadcast_to(row, (LANES, row.shape[1])).T


def forward_near_kernel(
    heads, own_ref, q_ref, k_ref, v_ref, seg_ref, e_ref, acc_ref, stat_ref, qa_scr, ka_scr, va_scr, stat_scr
):
    head = pl.program_id(0)
    rows = q_ref.shape[0]

    @pl.when(head == 0)
    def _():
        same = as_columns(seg_ref[pl.ds(own_ref[0], 1), :]) == lane_of((rows, LANES)).astype(F32)
        qa_scr[:, DH:] = jnp.where(same, 1.0, 0.0).astype(BF16)
        ka_scr[:, DH:] = jnp.where(same, 0.0, -BIG).astype(BF16)
        va_scr[:, DH:] = jnp.ones((rows, LANES), BF16)

    qa_scr[:, :DH] = q_ref[...]
    ka_scr[:, :DH] = k_ref[...]
    va_scr[:, :DH] = v_ref[...]

    def weigh(parts, pick):
        every = [dot_nt(qa_scr[part, :], ka_scr[...]) for part in parts]
        return every, [pick(part, logits) for part, logits in zip(parts, every)]

    def expose(parts, every, shifts):
        for part, logits, shift in zip(parts, every, shifts):
            e_ref[0, part, :] = jnp.exp2((logits - shift) * EXP2_SCALE).astype(BF16)

    def mix(parts, shifts):
        lane = lane_of((TQ, LANES))
        sums = []
        for part, shift in zip(parts, shifts):
            mixed = dot_nn(e_ref[0, part, :], va_scr[...])
            acc_ref[0, part, :] = mixed[:, :DH]
            kept = jnp.where(lane == head + heads, mixed[:, DH:], stat_scr[part, :])
            stat_scr[part, :] = jnp.where(lane == head, shift, kept)
            sums.append(mixed[:, DH:])
        return sums

    def own_logit(part, logits):
        return jnp.sum(q_ref[part, :].astype(F32) * k_ref[part, :].astype(F32), axis=1, keepdims=True)

    def top_logit(part, logits):
        return jnp.max(logits, axis=1, keepdims=True)

    sums, waiting = [], None
    for start in range(0, rows, GROUP * TQ):
        parts = [pl.ds(start + index * TQ, TQ) for index in range(GROUP)]
        every, shifts = weigh(parts, own_logit)
        if waiting is not None:
            sums += mix(*waiting)
        expose(parts, every, shifts)
        waiting = (parts, shifts)
    sums += mix(*waiting)
    safe = jnp.max(functools.reduce(jnp.maximum, sums)) <= SUM_LIMIT

    @pl.when(jnp.logical_not(safe))
    def _():
        @pl.loop(0, rows // TQ)
        def _(index):
            parts = [pl.ds(pl.multiple_of(index * TQ, TQ), TQ)]
            every, shifts = weigh(parts, top_logit)
            expose(parts, every, shifts)
            mix(parts, shifts)

    @pl.when(head == pl.num_programs(0) - 1)
    def _():
        stat_ref[...] = stat_scr[...].T[: 2 * heads, :]


def split_parts(x, count):
    parts = []
    for _ in range(count):
        piece = x.astype(BF16)
        parts.append(piece)
        x = x - piece.astype(F32)
    return parts


def row_sums(x, count):
    ones = jnp.ones((16, x.shape[1]), BF16)
    return sum(dot_nt(ones, piece) for piece in split_parts(x, count))[0:1, :]


def pair_columns(first, second):
    pieces = split_parts(first, 3) + split_parts(second, 3)
    rows = jnp.concatenate(pieces + [jnp.zeros((10, first.shape[1]), BF16)], axis=0)
    source = lax.broadcasted_iota(jnp.int32, (16, 2 * LANES), 0)
    lane = lane_of((16, 2 * LANES))
    spread = jnp.where((source < 3) == (lane < LANES), 1.0, 0.0).astype(BF16)
    wide = dot_tn(rows, spread)
    return wide[:, :LANES], wide[:, LANES:]


def forward_far_kernel(
    heads, levels, per, own_ref, off_ref, mask_ref, q_ref, seg_ref, acc_ref, stat_ref, og_ref, gain_ref, *rest
):
    recv = rest[:levels]
    att_ref, ef_ref, rate_ref, sums_ref, open_scr = rest[levels : levels + 5]
    seg_scr = rest[levels + 5 :]
    step = pl.program_id(0)
    rows = q_ref.shape[0]
    picks = rows // RATE
    tiles = mask_ref.shape[0]
    tile = rows // tiles

    @pl.when(step == 0)
    def _():
        sums_ref[...] = jnp.zeros_like(sums_ref)
        own = own_ref[0]
        own_row = seg_ref[pl.ds(own, 1), :]
        for level in range(levels):
            other = jnp.bitwise_xor(own, 2**level)
            seg_scr[level][...] = as_columns(seg_ref[pl.ds(other, 1), :])
            for index in range(tiles):
                span = slice(index * tile, (index + 1) * tile)
                shut = jnp.where(mask_ref[index, level] == 1, 0.0, 1.0)
                open_scr[level : level + 1, span] = own_row[:, span] - 1000.0 * shut

    subs = range(per)
    scores, sums = [], []
    for sub in subs:
        found = []
        for level in range(levels):
            picked = seg_scr[level][pl.ds(off_ref[level, step * per + sub], picks, stride=RATE), :]
            same = jnp.concatenate([picked] * (rows // LANES), axis=1) == open_scr[level : level + 1, :]
            part = dot_nt(recv[level][sub, 0], lanes(q_ref, sub)[...])
            found.append(jnp.where(same, part, -BIG))
        scores.append(found)
    tops = [functools.reduce(jnp.maximum, [jnp.max(x, axis=0, keepdims=True) for x in found]) for found in scores]
    for sub in subs:
        for level in range(levels):
            expo = jnp.exp2((scores[sub][level] - tops[sub]) * EXP2_SCALE).astype(BF16)
            ef_ref[sub, level * picks : (level + 1) * picks, :] = expo
    mixes = []
    for sub in subs:
        values = jnp.concatenate([ref[sub, 1] for ref in recv], axis=0)
        mixes.append(dot_tn(ef_ref[sub], values))
        ones = jnp.ones((16, levels * picks), BF16)
        sums.append(dot_nn(ones, ef_ref[sub])[0:1, :])
    columns = []
    for sub in subs:
        head = step * per + sub
        top_near = stat_ref[pl.ds(head, 1), :]
        sum_near = stat_ref[pl.ds(head + heads, 1), :]
        top = jnp.maximum(top_near, tops[sub])
        a_near = jnp.exp2((top_near - top) * EXP2_SCALE)
        a_far = jnp.exp2((tops[sub] - top) * EXP2_SCALE)
        inv = 1.0 / (a_near * sum_near + a_far * sums[sub])
        r_near = a_near * inv
        r_far = a_far * inv
        rate_ref[pl.ds(head, 1), :] = r_near
        rate_ref[pl.ds(head + heads, 1), :] = r_far
        columns.append(pair_columns(r_near, r_far))
    squares, crosses = [], []
    for sub in subs:
        att = columns[sub][0] * acc_ref[sub] + columns[sub][1] * mixes[sub]
        att_ref[sub] = att
        scaled = lanes(og_ref, sub)[...].astype(F32) * lanes(gain_ref, sub)[...]
        squares.append(att * att)
        crosses.append(scaled * att)
    sums_ref[0:1, :] += row_sums(functools.reduce(jnp.add, squares), 2)
    sums_ref[1:2, :] += row_sums(functools.reduce(jnp.add, crosses), 2)


def backward_far_kernel(heads, levels, per, width, parts, *refs):
    gathered = refs[:parts]
    att_ref, og_ref, gain_ref, rate_ref, q_ref, ef_ref = refs[parts : parts + 6]
    rest = refs[parts + 6 :]
    recv = rest[:levels]
    normed_ref, ga_ref, delta_ref, dq_ref = rest[levels : levels + 4]
    outs = rest[levels + 4 : levels + 4 + levels]
    inv_scr, cc_scr, gf_scr, gl_scr = rest[levels + 4 + levels :]
    step = pl.program_id(0)
    rows = q_ref.shape[0]
    picks = rows // RATE

    @pl.when(step == 0)
    def _():
        sums = functools.reduce(jnp.add, [ref[...] for ref in gathered])
        inv_row = lax.rsqrt(sums[0:1, :] / width + EPS)
        inv_scr[...] = as_columns(inv_row)
        cc_scr[...] = as_columns(inv_row * inv_row * (sums[1:2, :] / width))

    subs = range(per)
    deltas = []
    for sub in subs:
        head = step * per + sub
        near_col, far_col = pair_columns(rate_ref[pl.ds(head, 1), :], rate_ref[pl.ds(head + heads, 1), :])
        gain = lanes(gain_ref, sub)[...]
        att = att_ref[sub]
        inv = inv_scr[...]
        lanes(normed_ref, sub)[...] = (att * inv * gain).astype(BF16)
        scaled = lanes(og_ref, sub)[...].astype(F32) * gain
        grad_att = inv * (scaled - att * cc_scr[...])
        ga_near = (grad_att * near_col).astype(BF16)
        ga_far = (grad_att * far_col).astype(BF16)
        ga_ref[sub] = ga_near
        gf_scr[sub] = ga_far
        delta_near = jnp.sum(ga_near.astype(F32) * att, axis=1, keepdims=True)
        delta_ref[sub] = jnp.broadcast_to(delta_near, (rows, LANES))
        deltas.append(jnp.sum((ga_far.astype(F32) * att).T, axis=0, keepdims=True))
    for sub in subs:
        for level in range(levels):
            span = slice(level * picks, (level + 1) * picks)
            grad_w = dot_nt(recv[level][sub, 1], gf_scr[sub])
            gl_scr[sub, span, :] = (ef_ref[sub, span, :].astype(F32) * (grad_w - deltas[sub])).astype(BF16)
    for sub in subs:
        keys = jnp.concatenate([ref[sub, 0] for ref in recv], axis=0)
        dq_ref[sub] = dot_tn(gl_scr[sub], keys)
        dk = dot_nn(gl_scr[sub], lanes(q_ref, sub)[...]) * SCALE
        dv = dot_nn(ef_ref[sub], gf_scr[sub])
        for level, out in enumerate(outs):
            out[sub, 0] = dk[level * picks : (level + 1) * picks].astype(BF16)
            out[sub, 1] = dv[level * picks : (level + 1) * picks].astype(BF16)


def fold(wide, far):
    return ((wide[:, :DH] + wide[:, DH:] + far) * SCALE).astype(BF16)


def backward_near_kernel(e_ref, ga_ref, delta_ref, q_ref, k_ref, v_ref, dqf_ref, dq_ref, dk_ref, dv_ref, gl_scr, k_scr, qg_scr):
    rows = q_ref.shape[0]

    @pl.when(pl.program_id(0) == 0)
    def _():
        k_scr[:, DH:] = jnp.zeros((rows, DH), BF16)

    k_scr[:, :DH] = k_ref[...]
    qg_scr[:, :DH] = q_ref[...]
    qg_scr[:, DH:] = ga_ref[0]
    waiting = []
    for start in range(0, rows, TQ):
        part = pl.ds(start, TQ)
        grad_w = dot_nt(ga_ref[0, part, :], v_ref[...])
        for done in waiting:
            dq_ref[done, :] = fold(dot_nn(gl_scr[done, :], k_scr[...]), dqf_ref[0, done, :])
        delta = jnp.concatenate([delta_ref[0, part, :]] * (rows // LANES), axis=1)
        gl_scr[part, :] = (e_ref[0, part, :].astype(F32) * (grad_w - delta)).astype(BF16)
        waiting = [part]
    for done in waiting:
        dq_ref[done, :] = fold(dot_nn(gl_scr[done, :], k_scr[...]), dqf_ref[0, done, :])
    dk_ref[0] = dot_nn(q_ref[...].T, gl_scr[...]).T * SCALE
    dv_ref[0] = dot_nn(ga_ref[0].T, e_ref[0]).T


def merge_kernel(levels, per, off_ref, dk_ref, dv_ref, *rest):
    back = rest[:levels]
    gk_ref, gv_ref, k_scr, v_scr = rest[levels:]
    step = pl.program_id(0)
    picks = dk_ref.shape[1] // RATE
    for sub in range(per):
        k_scr[...] = dk_ref[sub]
        v_scr[...] = dv_ref[sub]
        for level in range(levels):
            spot = pl.ds(off_ref[level, step * per + sub], picks, stride=RATE)
            k_scr[spot, :] += back[level][sub, 0].astype(F32)
            v_scr[spot, :] += back[level][sub, 1].astype(F32)
        lanes(gk_ref, sub)[...] = k_scr[...].astype(BF16)
        lanes(gv_ref, sub)[...] = v_scr[...].astype(BF16)


def local(queries, key_rows, value_rows, out_grad, norm_gain, offsets, segments, tile_mask):
    rows = queries.shape[0]
    blocks = lax.axis_size("ctx")
    seg_rows = segments.reshape(blocks, rows)
    width = queries.shape[1]
    heads = width // DH
    picks = rows // RATE
    per = 4 if heads % 4 == 0 else 1
    smem = pl.BlockSpec(memory_space=pltpu.SMEM)
    wide = pl.BlockSpec((rows, per * DH), lambda h: (0, h))
    pair = pl.BlockSpec((per, 2, picks, DH), lambda h: (h, 0, 0, 0))
    pair_shape = jax.ShapeDtypeStruct((heads, 2, picks, DH), BF16)
    branch, *samples = pl.pallas_call(
        functools.partial(sample_kernel, per, blocks, rows),
        name="sample",
        grid=(heads // per,),
        in_specs=[smem, smem, wide, wide],
        out_specs=[smem] + [pair] * LEVELS,
        out_shape=[jax.ShapeDtypeStruct((1,), jnp.int32)] + [pair_shape] * LEVELS,
        scratch_shapes=[pltpu.VMEM((rows, DH), F32)] * 2,
        compiler_params=pltpu.CompilerParams(dimension_semantics=("arbitrary",), vmem_limit_bytes=12 << 20),
        cost_estimate=pl.CostEstimate(flops=0, bytes_accessed=6 * rows * width, transcendentals=0),
    )(segments, offsets, *(pltpu.with_memory_space_constraint(x, pltpu.HBM) for x in (key_rows, value_rows)))
    own = lax.axis_index("ctx").reshape(1)
    args = (queries, key_rows, value_rows, out_grad, norm_gain, offsets, seg_rows.astype(F32), tile_mask, own, samples)
    return lax.switch(branch[0], [functools.partial(layer, count + 1) for count in range(LEVELS)], *args)


def layer(levels, queries, key_rows, value_rows, out_grad, norm_gain, offsets, seg_rows, tile_mask, own, samples):
    rows, width = queries.shape
    blocks = seg_rows.shape[0]
    heads = width // DH
    picks = rows // RATE
    total_width = width * lax.axis_size("head")
    queries, key_rows, value_rows, out_grad = [
        pltpu.with_memory_space_constraint(x, pltpu.HBM) for x in (queries, key_rows, value_rows, out_grad)
    ]

    by_head = pl.BlockSpec((rows, DH), lambda h: (0, h))
    seg_spec = pl.BlockSpec((blocks, rows), lambda h: (0, 0))
    pair = pl.BlockSpec((1, 2, picks, DH), lambda h: (h, 0, 0, 0))
    major = pl.BlockSpec((1, rows, DH), lambda h: (h, 0, 0))
    major_f = jax.ShapeDtypeStruct((heads, rows, DH), F32)
    major_b = jax.ShapeDtypeStruct((heads, rows, DH), BF16)
    per = 2 if heads % 2 == 0 else 1
    wide_n = pl.BlockSpec((rows, per * DH), lambda h: (0, h))
    major_n = pl.BlockSpec((per, rows, DH), lambda h: (h, 0, 0))
    pair_n = pl.BlockSpec((per, 2, picks, DH), lambda h: (h, 0, 0, 0))
    stat_rows = pl.BlockSpec((2 * heads, rows), lambda h: (0, 0))
    smem = pl.BlockSpec(memory_space=pltpu.SMEM)
    gain_row = norm_gain.reshape(1, width)
    gain_spec = pl.BlockSpec((1, per * DH), lambda h: (0, h))

    def call(kernel, name, mib, in_specs, out_specs, out_shape, scratch=(), flops=0, moved=0, expo=0, per=1):
        return pl.pallas_call(
            kernel,
            name=name,
            grid=(heads // per,),
            in_specs=in_specs,
            out_specs=out_specs,
            out_shape=out_shape,
            scratch_shapes=scratch,
            compiler_params=pltpu.CompilerParams(dimension_semantics=("arbitrary",), vmem_limit_bytes=mib << 20),
            cost_estimate=pl.CostEstimate(flops=flops, bytes_accessed=moved, transcendentals=expo),
        )

    def shape(dims, dtype):
        return jax.ShapeDtypeStruct(dims, dtype)

    full = rows * width
    pair_shape = shape((heads, 2, picks, DH), BF16)
    recv = [partner(samples[level], "ctx", level) for level in range(levels)]

    square = rows * rows * heads
    expo, acc, stat = call(
        functools.partial(forward_near_kernel, heads),
        "forward_near",
        12,
        [smem, by_head, by_head, by_head, seg_spec],
        [pl.BlockSpec((1, rows, rows), lambda h: (h, 0, 0)), major, stat_rows],
        [pltpu.HBM((heads, rows, rows), BF16), major_f, shape((2 * heads, rows), F32)],
        [pltpu.VMEM((rows, 2 * DH), BF16)] * 3 + [pltpu.VMEM((rows, LANES), F32)],
        flops=4 * square * DH,
        moved=2 * square + 10 * full,
        expo=square,
    )(own, queries, key_rows, value_rows, seg_rows)

    far_n = levels * picks
    far_spec = pl.BlockSpec((per, far_n, rows), lambda h: (h, 0, 0))
    far_square = rows * far_n * heads
    att, expo_far, rate, sums = call(
        functools.partial(forward_far_kernel, heads, levels, per),
        "forward_far",
        18,
        [smem, smem, smem, wide_n, seg_spec, major_n, stat_rows, wide_n, gain_spec]
        + [pair_n] * levels,
        [major_n, far_spec, stat_rows, pl.BlockSpec((2, rows), lambda h: (0, 0))],
        [major_f, shape((heads, far_n, rows), BF16), shape((2 * heads, rows), F32), shape((2, rows), F32)],
        [pltpu.VMEM((levels, rows), F32)]
        + [pltpu.VMEM((rows, LANES), F32)] * levels,
        flops=4 * far_square * DH,
        moved=2 * far_square + 12 * full,
        per=per,
        expo=far_square,
    )(own, offsets, tile_mask, queries, seg_rows, acc, stat, out_grad, gain_row, *recv)
    parts = lax.axis_size("head")
    shifted = [
        lax.ppermute(sums, "head", [(i, (i + step) % parts) for i in range(parts)]) for step in range(1, parts)
    ]
    gathered = [sums] + shifted

    outs = call(
        functools.partial(backward_far_kernel, heads, levels, per, total_width, parts),
        "backward_far",
        18,
        [pl.BlockSpec((2, rows), lambda h: (0, 0))] * parts
        + [major_n, wide_n, gain_spec, stat_rows, wide_n, far_spec]
        + [pair_n] * levels,
        [wide_n, major_n, major_n, major_n] + [pair_n] * levels,
        [shape((rows, width), BF16), major_b, major_f, major_f]
        + [pair_shape] * levels,
        [pltpu.VMEM((rows, LANES), F32)] * 2
        + [pltpu.VMEM((per, rows, DH), BF16), pltpu.VMEM((per, far_n, rows), BF16)],
        flops=8 * far_square * DH,
        moved=2 * far_square + 16 * full,
        per=per,
    )(*gathered, att, out_grad, gain_row, rate, queries, expo_far, *recv)
    normed, grad_att, delta, dq_far = outs[:4]
    back = [partner(outs[4 + level], "ctx", level) for level in range(levels)]

    grad_queries, dk, dv = call(
        backward_near_kernel,
        "backward_near",
        20,
        [pl.BlockSpec((1, rows, rows), lambda h: (h, 0, 0)), major, major, by_head, by_head, by_head, major],
        [by_head, major, major],
        [shape((rows, width), BF16), major_f, major_f],
        [pltpu.VMEM((rows, rows), BF16)] + [pltpu.VMEM((rows, 2 * DH), BF16)] * 2,
        flops=8 * square * DH,
        moved=2 * square + 22 * full,
    )(pltpu.with_memory_space_constraint(expo, pltpu.HBM), grad_att, delta, queries, key_rows, value_rows, dq_far)

    grad_keys, grad_values = call(
        functools.partial(merge_kernel, levels, per),
        "merge",
        11,
        [smem, major_n, major_n] + [pair_n] * levels,
        [wide_n, wide_n],
        [shape((rows, width), BF16)] * 2,
        [pltpu.VMEM((rows, DH), F32)] * 2,
        moved=14 * full,
        per=per,
    )(offsets, dk, dv, *back)
    return (normed, grad_queries, grad_keys, grad_values)


def solution(mesh):
    placed = (
        P("ctx", "head"),
        P("ctx", "head"),
        P("ctx", "head"),
        P("ctx", "head"),
        P("head"),
        P(None, "head"),
        P(),
        P("ctx", None),
    )
    return jax.shard_map(
        local,
        mesh=mesh,
        in_specs=placed,
        out_specs=(P("ctx", "head"), P("ctx", "head"), P("ctx", "head"), P("ctx", "head")),
        check_vma=False,
    )
```

```python
import functools

import jax
import jax.numpy as jnp
from jax import lax
from jax.experimental import pallas as pl
from jax.experimental.pallas import tpu as pltpu
from jax.sharding import PartitionSpec as P

DH = 128
RATE = 8
LEVELS = 3
LANES = 128
BIG = 1e30
EPS = 1e-06
TQ = 256
GROUP = 2
SUM_LIMIT = 2.0**60
F32 = jnp.float32
BF16 = jnp.bfloat16
SCALE = DH ** (-0.5)
EXP2_SCALE = SCALE * 1.4426950408889634


def partner(value, axis, bit):
    mask = 2**bit
    pairs = [(source, source ^ mask) for source in range(lax.axis_size(axis))]
    return lax.ppermute(value, axis, pairs)


def dot_nt(a, b):
    return lax.dot_general(a, b, (((1,), (1,)), ((), ())), preferred_element_type=F32)


def dot_nn(a, b):
    return lax.dot_general(a, b, (((1,), (0,)), ((), ())), preferred_element_type=F32)


def dot_tn(a, b):
    return lax.dot_general(a, b, (((0,), (0,)), ((), ())), preferred_element_type=F32)


def lane_of(shape):
    return lax.broadcasted_iota(jnp.int32, shape, 1)


def lanes(ref, sub):
    return ref.at[:, pl.ds(sub * DH, DH)]


def lead(ref, sub):
    return ref.at[pl.ds(sub, 1)]


def sample_kernel(per, blocks, rows, seg_ref, off_ref, k_ref, v_ref, branch_ref, *rest):
    outs, (k_scr, v_scr) = rest[:-2], rest[-2:]
    step = pl.program_id(0)
    picks = rows // RATE

    @pl.when(step == 0)
    def _():
        first = [seg_ref[block * rows] for block in range(blocks)]
        last = [seg_ref[block * rows + rows - 1] for block in range(blocks)]
        branch = jnp.int32(0)
        for level in range(1, LEVELS):
            meet = jnp.int32(0)
            for block in range(blocks):
                other = block ^ 2**level
                if block < other:
                    near = jnp.maximum(first[block], first[other]) <= jnp.minimum(last[block], last[other])
                    meet = jnp.where(near, jnp.int32(1), meet)
            branch = jnp.where(meet == 1, jnp.int32(level), branch)
        branch_ref[0] = branch

    for sub in range(per):
        k_scr[...] = lanes(k_ref, sub)[...].astype(F32)
        v_scr[...] = lanes(v_ref, sub)[...].astype(F32)
        for level, out in enumerate(outs):
            start = off_ref[level, step * per + sub]
            out[sub, 0] = k_scr[pl.ds(start, picks, stride=RATE), :].astype(BF16)
            out[sub, 1] = v_scr[pl.ds(start, picks, stride=RATE), :].astype(BF16)


def as_columns(row):
    return jnp.broadcast_to(row, (LANES, row.shape[1])).T


def forward_near_kernel(
    heads, own_ref, q_ref, k_ref, v_ref, seg_ref, e_ref, acc_ref, stat_ref, qa_scr, ka_scr, va_scr, stat_scr
):
    head = pl.program_id(0)
    rows = q_ref.shape[0]

    @pl.when(head == 0)
    def _():
        same = as_columns(segment_row(seg_ref, own_ref[0], rows)) == lane_of((rows, LANES)).astype(F32)
        qa_scr[:, DH:] = jnp.where(same, 1.0, 0.0).astype(BF16)
        ka_scr[:, DH:] = jnp.where(same, 0.0, -BIG).astype(BF16)
        va_scr[:, DH:] = jnp.ones((rows, LANES), BF16)

    qa_scr[:, :DH] = q_ref[...]
    ka_scr[:, :DH] = k_ref[...]
    va_scr[:, :DH] = v_ref[...]

    def weigh(parts, pick):
        every = [dot_nt(qa_scr[part, :], ka_scr[...]) for part in parts]
        return every, [pick(part, logits) for part, logits in zip(parts, every)]

    def expose(parts, every, shifts):
        for part, logits, shift in zip(parts, every, shifts):
            e_ref[0, part, :] = jnp.exp2((logits - shift) * EXP2_SCALE).astype(BF16)

    def mix(parts, shifts):
        lane = lane_of((TQ, LANES))
        sums = []
        for part, shift in zip(parts, shifts):
            mixed = dot_nn(e_ref[0, part, :], va_scr[...])
            acc_ref[0, part, :] = mixed[:, :DH]
            kept = jnp.where(lane == head + heads, mixed[:, DH:], stat_scr[part, :])
            stat_scr[part, :] = jnp.where(lane == head, shift, kept)
            sums.append(mixed[:, DH:])
        return sums

    def own_logit(part, logits):
        return jnp.sum(q_ref[part, :].astype(F32) * k_ref[part, :].astype(F32), axis=1, keepdims=True)

    def top_logit(part, logits):
        return jnp.max(logits, axis=1, keepdims=True)

    sums, waiting = [], None
    for start in range(0, rows, GROUP * TQ):
        parts = [pl.ds(start + index * TQ, TQ) for index in range(GROUP)]
        every, shifts = weigh(parts, own_logit)
        if waiting is not None:
            sums += mix(*waiting)
        expose(parts, every, shifts)
        waiting = (parts, shifts)
    sums += mix(*waiting)
    safe = jnp.max(functools.reduce(jnp.maximum, sums)) <= SUM_LIMIT

    @pl.when(jnp.logical_not(safe))
    def _():
        @pl.loop(0, rows // TQ)
        def _(index):
            parts = [pl.ds(pl.multiple_of(index * TQ, TQ), TQ)]
            every, shifts = weigh(parts, top_logit)
            expose(parts, every, shifts)
            mix(parts, shifts)

    @pl.when(head == pl.num_programs(0) - 1)
    def _():
        stat_ref[...] = stat_scr[...].T[: 2 * heads, :]


def segment_row(ref, block, rows):
    depth = rows // LANES
    part = ref[pl.ds(pl.multiple_of(block * depth, depth), depth), :].astype(F32)
    return jnp.concatenate([part[i : i + 1, :] for i in range(depth)], axis=1)


def split_parts(x, count):
    parts = []
    for _ in range(count):
        piece = x.astype(BF16)
        parts.append(piece)
        x = x - piece.astype(F32)
    return parts


def row_sums(x, count):
    ones = jnp.ones((16, x.shape[1]), BF16)
    return sum(dot_nt(ones, piece) for piece in split_parts(x, count))[0:1, :]


def pair_columns(first, second):
    pieces = split_parts(first, 3) + split_parts(second, 3)
    rows = jnp.concatenate(pieces + [jnp.zeros((10, first.shape[1]), BF16)], axis=0)
    source = lax.broadcasted_iota(jnp.int32, (16, 2 * LANES), 0)
    lane = lane_of((16, 2 * LANES))
    spread = jnp.where((source < 3) == (lane < LANES), 1.0, 0.0).astype(BF16)
    wide = dot_tn(rows, spread)
    return wide[:, :LANES], wide[:, LANES:]


def forward_far_kernel(
    heads, levels, per, own_ref, off_ref, mask_ref, q_ref, seg_ref, acc_ref, stat_ref, og_ref, gain_ref, *rest
):
    recv = rest[:levels]
    att_ref, ef_ref, rate_ref, sums_ref, open_scr = rest[levels : levels + 5]
    seg_scr = rest[levels + 5 :]
    step = pl.program_id(0)
    rows = q_ref.shape[0]
    picks = rows // RATE
    tiles = mask_ref.shape[0]
    tile = rows // tiles

    @pl.when(step == 0)
    def _():
        sums_ref[...] = jnp.zeros_like(sums_ref)
        own = own_ref[0]
        own_row = segment_row(seg_ref, own, rows)
        for level in range(levels):
            other = jnp.bitwise_xor(own, 2**level)
            seg_scr[level][...] = as_columns(segment_row(seg_ref, other, rows))
            for index in range(tiles):
                span = slice(index * tile, (index + 1) * tile)
                shut = jnp.where(mask_ref[index, level] == 1, 0.0, 1.0)
                open_scr[level : level + 1, span] = own_row[:, span] - 1000.0 * shut

    subs = range(per)
    scores, sums = [], []
    for sub in subs:
        found = []
        for level in range(levels):
            picked = seg_scr[level][pl.ds(off_ref[level, step * per + sub], picks, stride=RATE), :]
            same = jnp.concatenate([picked] * (rows // LANES), axis=1) == open_scr[level : level + 1, :]
            part = dot_nt(recv[level][sub, 0], lanes(q_ref, sub)[...])
            found.append(jnp.where(same, part, -BIG))
        scores.append(found)
    tops = [functools.reduce(jnp.maximum, [jnp.max(x, axis=0, keepdims=True) for x in found]) for found in scores]
    for sub in subs:
        for level in range(levels):
            expo = jnp.exp2((scores[sub][level] - tops[sub]) * EXP2_SCALE).astype(BF16)
            ef_ref[sub, level * picks : (level + 1) * picks, :] = expo
    mixes = []
    for sub in subs:
        values = jnp.concatenate([ref[sub, 1] for ref in recv], axis=0)
        mixes.append(dot_tn(ef_ref[sub], values))
        ones = jnp.ones((16, levels * picks), BF16)
        sums.append(dot_nn(ones, ef_ref[sub])[0:1, :])
    columns = []
    for sub in subs:
        head = step * per + sub
        top_near = stat_ref[pl.ds(head, 1), :]
        sum_near = stat_ref[pl.ds(head + heads, 1), :]
        top = jnp.maximum(top_near, tops[sub])
        a_near = jnp.exp2((top_near - top) * EXP2_SCALE)
        a_far = jnp.exp2((tops[sub] - top) * EXP2_SCALE)
        inv = 1.0 / (a_near * sum_near + a_far * sums[sub])
        r_near = a_near * inv
        r_far = a_far * inv
        rate_ref[pl.ds(head, 1), :] = r_near
        rate_ref[pl.ds(head + heads, 1), :] = r_far
        columns.append(pair_columns(r_near, r_far))
    squares, crosses = [], []
    for sub in subs:
        att = columns[sub][0] * acc_ref[sub] + columns[sub][1] * mixes[sub]
        att_ref[sub] = att
        scaled = lanes(og_ref, sub)[...].astype(F32) * lanes(gain_ref, sub)[...]
        squares.append(att * att)
        crosses.append(scaled * att)
    sums_ref[0:1, :] += row_sums(functools.reduce(jnp.add, squares), 2)
    sums_ref[1:2, :] += row_sums(functools.reduce(jnp.add, crosses), 2)


def backward_far_kernel(heads, levels, per, width, parts, *refs):
    gathered = refs[:parts]
    att_ref, og_ref, gain_ref, rate_ref, q_ref, ef_ref = refs[parts : parts + 6]
    rest = refs[parts + 6 :]
    recv = rest[:levels]
    normed_ref, ga_ref, delta_ref, dq_ref = rest[levels : levels + 4]
    outs = rest[levels + 4 : levels + 4 + levels]
    inv_scr, cc_scr, gf_scr, gl_scr = rest[levels + 4 + levels :]
    step = pl.program_id(0)
    rows = q_ref.shape[0]
    picks = rows // RATE

    @pl.when(step == 0)
    def _():
        sums = functools.reduce(jnp.add, [ref[...] for ref in gathered])
        inv_row = lax.rsqrt(sums[0:1, :] / width + EPS)
        inv_scr[...] = as_columns(inv_row)
        cc_scr[...] = as_columns(inv_row * inv_row * (sums[1:2, :] / width))

    subs = range(per)
    deltas = []
    for sub in subs:
        head = step * per + sub
        near_col, far_col = pair_columns(rate_ref[pl.ds(head, 1), :], rate_ref[pl.ds(head + heads, 1), :])
        gain = lanes(gain_ref, sub)[...]
        att = att_ref[sub]
        inv = inv_scr[...]
        lanes(normed_ref, sub)[...] = (att * inv * gain).astype(BF16)
        scaled = lanes(og_ref, sub)[...].astype(F32) * gain
        grad_att = inv * (scaled - att * cc_scr[...])
        ga_near = (grad_att * near_col).astype(BF16)
        ga_far = (grad_att * far_col).astype(BF16)
        ga_ref[sub] = ga_near
        gf_scr[sub] = ga_far
        delta_near = jnp.sum(ga_near.astype(F32) * att, axis=1, keepdims=True)
        delta_ref[sub] = jnp.broadcast_to(delta_near, (rows, LANES))
        deltas.append(jnp.sum((ga_far.astype(F32) * att).T, axis=0, keepdims=True))
    for sub in subs:
        for level in range(levels):
            span = slice(level * picks, (level + 1) * picks)
            grad_w = dot_nt(recv[level][sub, 1], gf_scr[sub])
            gl_scr[sub, span, :] = (ef_ref[sub, span, :].astype(F32) * (grad_w - deltas[sub])).astype(BF16)
    for sub in subs:
        keys = jnp.concatenate([ref[sub, 0] for ref in recv], axis=0)
        dq_ref[sub] = dot_tn(gl_scr[sub], keys)
        dk = dot_nn(gl_scr[sub], lanes(q_ref, sub)[...]) * SCALE
        dv = dot_nn(ef_ref[sub], gf_scr[sub])
        for level, out in enumerate(outs):
            out[sub, 0] = dk[level * picks : (level + 1) * picks].astype(BF16)
            out[sub, 1] = dv[level * picks : (level + 1) * picks].astype(BF16)


def fold(wide, far):
    return ((wide[:, :DH] + wide[:, DH:] + far) * SCALE).astype(BF16)


def backward_near_kernel(e_ref, ga_ref, delta_ref, q_ref, k_ref, v_ref, dqf_ref, dq_ref, dk_ref, dv_ref, gl_scr, k_scr, qg_scr):
    rows = q_ref.shape[0]

    for start in range(0, rows, TQ):
        part = pl.ds(start, TQ)
        grad_w = dot_nt(ga_ref[0, part, :], v_ref[...])
        delta = jnp.concatenate([delta_ref[0, part, :]] * (rows // LANES), axis=1)
        gl_scr[part, :] = (e_ref[0, part, :].astype(F32) * (grad_w - delta)).astype(BF16)
    dv_ref[0] = dot_nn(ga_ref[0].T, e_ref[0]).T
    dq_ref[...] = ((dot_nn(gl_scr[...], k_ref[...]) + dqf_ref[0]) * SCALE).astype(BF16)
    dk_ref[0] = dot_tn(gl_scr[...], q_ref[...]) * SCALE


def merge_kernel(levels, per, off_ref, dk_ref, dv_ref, *rest):
    back = rest[:levels]
    gk_ref, gv_ref, k_scr, v_scr = rest[levels:]
    step = pl.program_id(0)
    picks = dk_ref.shape[1] // RATE
    for sub in range(per):
        k_scr[...] = dk_ref[sub]
        v_scr[...] = dv_ref[sub]
        for level in range(levels):
            spot = pl.ds(off_ref[level, step * per + sub], picks, stride=RATE)
            k_scr[spot, :] += back[level][sub, 0].astype(F32)
            v_scr[spot, :] += back[level][sub, 1].astype(F32)
        lanes(gk_ref, sub)[...] = k_scr[...].astype(BF16)
        lanes(gv_ref, sub)[...] = v_scr[...].astype(BF16)


def local(queries, key_rows, value_rows, out_grad, norm_gain, offsets, segments, tile_mask):
    rows = queries.shape[0]
    blocks = lax.axis_size("ctx")
    seg_rows = segments.reshape(-1, LANES)
    width = queries.shape[1]
    heads = width // DH
    picks = rows // RATE
    per = 4 if heads % 4 == 0 else 1
    smem = pl.BlockSpec(memory_space=pltpu.SMEM)
    wide = pl.BlockSpec((rows, per * DH), lambda h: (0, h))
    pair = pl.BlockSpec((per, 2, picks, DH), lambda h: (h, 0, 0, 0))
    pair_shape = jax.ShapeDtypeStruct((heads, 2, picks, DH), BF16)
    branch, *samples = pl.pallas_call(
        functools.partial(sample_kernel, per, blocks, rows),
        name="sample",
        grid=(heads // per,),
        in_specs=[smem, smem, wide, wide],
        out_specs=[smem] + [pair] * LEVELS,
        out_shape=[jax.ShapeDtypeStruct((1,), jnp.int32)] + [pair_shape] * LEVELS,
        scratch_shapes=[pltpu.VMEM((rows, DH), F32)] * 2,
        compiler_params=pltpu.CompilerParams(dimension_semantics=("arbitrary",), vmem_limit_bytes=12 << 20),
        cost_estimate=pl.CostEstimate(flops=0, bytes_accessed=6 * rows * width, transcendentals=0),
    )(pltpu.with_memory_space_constraint(segments, pltpu.HBM), offsets, *(pltpu.with_memory_space_constraint(x, pltpu.HBM) for x in (key_rows, value_rows)))
    own = lax.axis_index("ctx").reshape(1)
    args = (queries, key_rows, value_rows, out_grad, norm_gain, offsets, seg_rows, tile_mask, own, samples)
    return lax.switch(branch[0], [functools.partial(layer, count + 1) for count in range(LEVELS)], *args)


def layer(levels, queries, key_rows, value_rows, out_grad, norm_gain, offsets, seg_rows, tile_mask, own, samples):
    rows, width = queries.shape
    heads = width // DH
    picks = rows // RATE
    total_width = width * lax.axis_size("head")
    queries, key_rows, value_rows, out_grad = [
        pltpu.with_memory_space_constraint(x, pltpu.HBM) for x in (queries, key_rows, value_rows, out_grad)
    ]

    by_head = pl.BlockSpec((rows, DH), lambda h: (0, h))
    seg_spec = pl.BlockSpec(seg_rows.shape, lambda h: (0, 0))
    pair = pl.BlockSpec((1, 2, picks, DH), lambda h: (h, 0, 0, 0))
    major = pl.BlockSpec((1, rows, DH), lambda h: (h, 0, 0))
    major_f = jax.ShapeDtypeStruct((heads, rows, DH), F32)
    major_b = jax.ShapeDtypeStruct((heads, rows, DH), BF16)
    per = 2 if heads % 2 == 0 else 1
    wide_n = pl.BlockSpec((rows, per * DH), lambda h: (0, h))
    major_n = pl.BlockSpec((per, rows, DH), lambda h: (h, 0, 0))
    pair_n = pl.BlockSpec((per, 2, picks, DH), lambda h: (h, 0, 0, 0))
    stat_rows = pl.BlockSpec((2 * heads, rows), lambda h: (0, 0))
    smem = pl.BlockSpec(memory_space=pltpu.SMEM)
    gain_row = norm_gain.reshape(1, width)
    gain_spec = pl.BlockSpec((1, per * DH), lambda h: (0, h))

    def call(kernel, name, mib, in_specs, out_specs, out_shape, scratch=(), flops=0, moved=0, expo=0, per=1):
        return pl.pallas_call(
            kernel,
            name=name,
            grid=(heads // per,),
            in_specs=in_specs,
            out_specs=out_specs,
            out_shape=out_shape,
            scratch_shapes=scratch,
            compiler_params=pltpu.CompilerParams(dimension_semantics=("arbitrary",), vmem_limit_bytes=mib << 20),
            cost_estimate=pl.CostEstimate(flops=flops, bytes_accessed=moved, transcendentals=expo),
        )

    def shape(dims, dtype):
        return jax.ShapeDtypeStruct(dims, dtype)

    full = rows * width
    pair_shape = shape((heads, 2, picks, DH), BF16)
    recv = [partner(samples[level], "ctx", level) for level in range(levels)]

    square = rows * rows * heads
    expo, acc, stat = call(
        functools.partial(forward_near_kernel, heads),
        "forward_near",
        12,
        [smem, by_head, by_head, by_head, seg_spec],
        [pl.BlockSpec((1, rows, rows), lambda h: (h, 0, 0)), major, stat_rows],
        [pltpu.HBM((heads, rows, rows), BF16), major_f, shape((2 * heads, rows), F32)],
        [pltpu.VMEM((rows, 2 * DH), BF16)] * 3 + [pltpu.VMEM((rows, LANES), F32)],
        flops=4 * square * DH,
        moved=2 * square + 10 * full,
        expo=square,
    )(own, queries, key_rows, value_rows, seg_rows)

    far_n = levels * picks
    far_spec = pl.BlockSpec((per, far_n, rows), lambda h: (h, 0, 0))
    far_square = rows * far_n * heads
    att, expo_far, rate, sums = call(
        functools.partial(forward_far_kernel, heads, levels, per),
        "forward_far",
        18,
        [smem, smem, smem, wide_n, seg_spec, major_n, stat_rows, wide_n, gain_spec]
        + [pair_n] * levels,
        [major_n, far_spec, stat_rows, pl.BlockSpec((2, rows), lambda h: (0, 0))],
        [major_f, shape((heads, far_n, rows), BF16), shape((2 * heads, rows), F32), shape((2, rows), F32)],
        [pltpu.VMEM((levels, rows), F32)]
        + [pltpu.VMEM((rows, LANES), F32)] * levels,
        flops=4 * far_square * DH,
        moved=2 * far_square + 12 * full,
        per=per,
        expo=far_square,
    )(own, offsets, tile_mask, queries, seg_rows, acc, stat, out_grad, gain_row, *recv)
    parts = lax.axis_size("head")
    shifted = [
        lax.ppermute(sums, "head", [(i, (i + step) % parts) for i in range(parts)]) for step in range(1, parts)
    ]
    gathered = [sums] + shifted

    outs = call(
        functools.partial(backward_far_kernel, heads, levels, per, total_width, parts),
        "backward_far",
        18,
        [pl.BlockSpec((2, rows), lambda h: (0, 0))] * parts
        + [major_n, wide_n, gain_spec, stat_rows, wide_n, far_spec]
        + [pair_n] * levels,
        [wide_n, major_n, major_n, major_n] + [pair_n] * levels,
        [shape((rows, width), BF16), major_b, major_f, major_f]
        + [pair_shape] * levels,
        [pltpu.VMEM((rows, LANES), F32)] * 2
        + [pltpu.VMEM((per, rows, DH), BF16), pltpu.VMEM((per, far_n, rows), BF16)],
        flops=8 * far_square * DH,
        moved=2 * far_square + 16 * full,
        per=per,
    )(*gathered, att, out_grad, gain_row, rate, queries, expo_far, *recv)
    normed, grad_att, delta, dq_far = outs[:4]
    back = [partner(outs[4 + level], "ctx", level) for level in range(levels)]

    grad_queries, dk, dv = call(
        backward_near_kernel,
        "backward_near",
        20,
        [pl.BlockSpec((1, rows, rows), lambda h: (h, 0, 0)), major, major, by_head, by_head, by_head, major],
        [by_head, major, major],
        [shape((rows, width), BF16), major_f, major_f],
        [pltpu.VMEM((rows, rows), BF16)] + [pltpu.VMEM((rows, 2 * DH), BF16)] * 2,
        flops=8 * square * DH,
        moved=2 * square + 22 * full,
    )(pltpu.with_memory_space_constraint(expo, pltpu.HBM), grad_att, delta, queries, key_rows, value_rows, dq_far)

    grad_keys, grad_values = call(
        functools.partial(merge_kernel, levels, per),
        "merge",
        11,
        [smem, major_n, major_n] + [pair_n] * levels,
        [wide_n, wide_n],
        [shape((rows, width), BF16)] * 2,
        [pltpu.VMEM((rows, DH), F32)] * 2,
        moved=14 * full,
        per=per,
    )(offsets, dk, dv, *back)
    return (normed, grad_queries, grad_keys, grad_values)


def solution(mesh):
    placed = (
        P("ctx", "head"),
        P("ctx", "head"),
        P("ctx", "head"),
        P("ctx", "head"),
        P("head"),
        P(None, "head"),
        P(),
        P("ctx", None),
    )
    return jax.shard_map(
        local,
        mesh=mesh,
        in_specs=placed,
        out_specs=(P("ctx", "head"), P("ctx", "head"), P("ctx", "head"), P("ctx", "head")),
        check_vma=False,
    )
```

```python
import functools

import jax
import jax.numpy as jnp
from jax import lax
from jax.experimental import pallas as pl
from jax.experimental.pallas import tpu as pltpu
from jax.sharding import PartitionSpec as P

DH = 128
RATE = 8
LEVELS = 3
LANES = 128
BIG = 1e30
EPS = 1e-06
TQ = 256
GROUP = 2
SUM_LIMIT = 2.0**60
F32 = jnp.float32
BF16 = jnp.bfloat16
SCALE = DH ** (-0.5)
EXP2_SCALE = SCALE * 1.4426950408889634


def partner(value, axis, bit):
    mask = 2**bit
    pairs = [(source, source ^ mask) for source in range(lax.axis_size(axis))]
    return lax.ppermute(value, axis, pairs)


def dot_nt(a, b):
    return lax.dot_general(a, b, (((1,), (1,)), ((), ())), preferred_element_type=F32)


def dot_nn(a, b):
    return lax.dot_general(a, b, (((1,), (0,)), ((), ())), preferred_element_type=F32)


def dot_tn(a, b):
    return lax.dot_general(a, b, (((0,), (0,)), ((), ())), preferred_element_type=F32)


def lane_of(shape):
    return lax.broadcasted_iota(jnp.int32, shape, 1)


def lanes(ref, sub):
    return ref.at[:, pl.ds(sub * DH, DH)]


def lead(ref, sub):
    return ref.at[pl.ds(sub, 1)]


def sample_kernel(per, blocks, rows, seg_ref, off_ref, k_ref, v_ref, branch_ref, *rest):
    outs, (k_scr, v_scr) = rest[:-2], rest[-2:]
    step = pl.program_id(0)
    picks = rows // RATE

    @pl.when(step == 0)
    def _():
        first = [seg_ref[block * rows] for block in range(blocks)]
        last = [seg_ref[block * rows + rows - 1] for block in range(blocks)]
        branch = jnp.int32(0)
        for level in range(1, LEVELS):
            meet = jnp.int32(0)
            for block in range(blocks):
                other = block ^ 2**level
                if block < other:
                    near = jnp.maximum(first[block], first[other]) <= jnp.minimum(last[block], last[other])
                    meet = jnp.where(near, jnp.int32(1), meet)
            branch = jnp.where(meet == 1, jnp.int32(level), branch)
        branch_ref[0] = branch

    for sub in range(per):
        k_scr[...] = lanes(k_ref, sub)[...].astype(F32)
        v_scr[...] = lanes(v_ref, sub)[...].astype(F32)
        for level, out in enumerate(outs):
            start = off_ref[level, step * per + sub]
            out[sub, 0] = k_scr[pl.ds(start, picks, stride=RATE), :].astype(BF16)
            out[sub, 1] = v_scr[pl.ds(start, picks, stride=RATE), :].astype(BF16)


def as_columns(row):
    return jnp.broadcast_to(row, (LANES, row.shape[1])).T


def forward_near_kernel(
    heads, own_ref, q_ref, k_ref, v_ref, seg_ref, e_ref, acc_ref, stat_ref, qa_scr, ka_scr, va_scr, stat_scr
):
    head = pl.program_id(0)
    rows = q_ref.shape[0]

    @pl.when(head == 0)
    def _():
        same = as_columns(segment_row(seg_ref, own_ref[0], rows)) == lane_of((rows, LANES)).astype(F32)
        qa_scr[:, DH:] = jnp.where(same, 1.0, 0.0).astype(BF16)
        ka_scr[:, DH:] = jnp.where(same, 0.0, -BIG).astype(BF16)
        va_scr[:, DH:] = jnp.ones((rows, LANES), BF16)

    qa_scr[:, :DH] = q_ref[...]
    ka_scr[:, :DH] = k_ref[...]
    va_scr[:, :DH] = v_ref[...]

    def weigh(parts, pick):
        every = [dot_nt(qa_scr[part, :], ka_scr[...]) for part in parts]
        return every, [pick(part, logits) for part, logits in zip(parts, every)]

    def expose(parts, every, shifts):
        for part, logits, shift in zip(parts, every, shifts):
            e_ref[0, part, :] = jnp.exp2((logits - shift) * EXP2_SCALE).astype(BF16)

    def mix(parts, shifts):
        lane = lane_of((TQ, LANES))
        sums = []
        for part, shift in zip(parts, shifts):
            mixed = dot_nn(e_ref[0, part, :], va_scr[...])
            acc_ref[0, part, :] = mixed[:, :DH]
            kept = jnp.where(lane == head + heads, mixed[:, DH:], stat_scr[part, :])
            stat_scr[part, :] = jnp.where(lane == head, shift, kept)
            sums.append(mixed[:, DH:])
        return sums

    def own_logit(part, logits):
        return jnp.sum(q_ref[part, :].astype(F32) * k_ref[part, :].astype(F32), axis=1, keepdims=True)

    def top_logit(part, logits):
        return jnp.max(logits, axis=1, keepdims=True)

    sums, waiting = [], None
    for start in range(0, rows, GROUP * TQ):
        parts = [pl.ds(start + index * TQ, TQ) for index in range(GROUP)]
        every, shifts = weigh(parts, own_logit)
        if waiting is not None:
            sums += mix(*waiting)
        expose(parts, every, shifts)
        waiting = (parts, shifts)
    sums += mix(*waiting)
    safe = jnp.max(functools.reduce(jnp.maximum, sums)) <= SUM_LIMIT

    @pl.when(jnp.logical_not(safe))
    def _():
        @pl.loop(0, rows // TQ)
        def _(index):
            parts = [pl.ds(pl.multiple_of(index * TQ, TQ), TQ)]
            every, shifts = weigh(parts, top_logit)
            expose(parts, every, shifts)
            mix(parts, shifts)

    @pl.when(head == pl.num_programs(0) - 1)
    def _():
        stat_ref[...] = stat_scr[...].T[: 2 * heads, :]


def segment_row(ref, block, rows):
    depth = rows // LANES
    part = ref[pl.ds(pl.multiple_of(block * depth, depth), depth), :].astype(F32)
    return jnp.concatenate([part[i : i + 1, :] for i in range(depth)], axis=1)


def split_parts(x, count):
    parts = []
    for _ in range(count):
        piece = x.astype(BF16)
        parts.append(piece)
        x = x - piece.astype(F32)
    return parts


def row_sums(x, count):
    ones = jnp.ones((16, x.shape[1]), BF16)
    return sum(dot_nt(ones, piece) for piece in split_parts(x, count))[0:1, :]


def pair_columns(first, second):
    pieces = split_parts(first, 3) + split_parts(second, 3)
    rows = jnp.concatenate(pieces + [jnp.zeros((10, first.shape[1]), BF16)], axis=0)
    source = lax.broadcasted_iota(jnp.int32, (16, 2 * LANES), 0)
    lane = lane_of((16, 2 * LANES))
    spread = jnp.where((source < 3) == (lane < LANES), 1.0, 0.0).astype(BF16)
    wide = dot_tn(rows, spread)
    return wide[:, :LANES], wide[:, LANES:]


def forward_far_kernel(
    heads, levels, per, own_ref, off_ref, mask_ref, q_ref, seg_ref, acc_ref, stat_ref, og_ref, gain_ref, *rest
):
    recv = rest[:levels]
    att_ref, ef_ref, rate_ref, sums_ref, open_scr = rest[levels : levels + 5]
    seg_scr = rest[levels + 5 :]
    step = pl.program_id(0)
    rows = q_ref.shape[0]
    picks = rows // RATE
    tiles = mask_ref.shape[0]
    tile = rows // tiles

    @pl.when(step == 0)
    def _():
        sums_ref[...] = jnp.zeros_like(sums_ref)
        own = own_ref[0]
        own_row = segment_row(seg_ref, own, rows)
        for level in range(levels):
            other = jnp.bitwise_xor(own, 2**level)
            seg_scr[level][...] = as_columns(segment_row(seg_ref, other, rows))
            for index in range(tiles):
                span = slice(index * tile, (index + 1) * tile)
                shut = jnp.where(mask_ref[index, level] == 1, 0.0, 1.0)
                open_scr[level : level + 1, span] = own_row[:, span] - 1000.0 * shut

    subs = range(per)
    scores, sums = [], []
    for sub in subs:
        found = []
        for level in range(levels):
            picked = seg_scr[level][pl.ds(off_ref[level, step * per + sub], picks, stride=RATE), :]
            same = jnp.concatenate([picked] * (rows // LANES), axis=1) == open_scr[level : level + 1, :]
            part = dot_nt(recv[level][sub, 0], lanes(q_ref, sub)[...])
            found.append(jnp.where(same, part, -BIG))
        scores.append(found)
    tops = [functools.reduce(jnp.maximum, [jnp.max(x, axis=0, keepdims=True) for x in found]) for found in scores]
    for sub in subs:
        for level in range(levels):
            expo = jnp.exp2((scores[sub][level] - tops[sub]) * EXP2_SCALE).astype(BF16)
            ef_ref[sub, level * picks : (level + 1) * picks, :] = expo
    mixes = []
    for sub in subs:
        values = jnp.concatenate([ref[sub, 1] for ref in recv], axis=0)
        mixes.append(dot_tn(ef_ref[sub], values))
        ones = jnp.ones((16, levels * picks), BF16)
        sums.append(dot_nn(ones, ef_ref[sub])[0:1, :])
    columns = []
    for sub in subs:
        head = step * per + sub
        top_near = stat_ref[pl.ds(head, 1), :]
        sum_near = stat_ref[pl.ds(head + heads, 1), :]
        top = jnp.maximum(top_near, tops[sub])
        a_near = jnp.exp2((top_near - top) * EXP2_SCALE)
        a_far = jnp.exp2((tops[sub] - top) * EXP2_SCALE)
        inv = 1.0 / (a_near * sum_near + a_far * sums[sub])
        r_near = a_near * inv
        r_far = a_far * inv
        rate_ref[pl.ds(head, 1), :] = r_near
        rate_ref[pl.ds(head + heads, 1), :] = r_far
        columns.append(pair_columns(r_near, r_far))
    squares, crosses = [], []
    for sub in subs:
        att = columns[sub][0] * acc_ref[sub] + columns[sub][1] * mixes[sub]
        att_ref[sub] = att
        scaled = lanes(og_ref, sub)[...].astype(F32) * lanes(gain_ref, sub)[...]
        squares.append(att * att)
        crosses.append(scaled * att)
    sums_ref[0:1, :] += row_sums(functools.reduce(jnp.add, squares), 2)
    sums_ref[1:2, :] += row_sums(functools.reduce(jnp.add, crosses), 2)


def backward_far_kernel(heads, levels, per, width, parts, *refs):
    gathered = refs[:parts]
    att_ref, og_ref, gain_ref, rate_ref, q_ref, ef_ref = refs[parts : parts + 6]
    rest = refs[parts + 6 :]
    recv = rest[:levels]
    normed_ref, ga_ref, delta_ref, dq_ref = rest[levels : levels + 4]
    outs = rest[levels + 4 : levels + 4 + levels]
    inv_scr, cc_scr, gf_scr, gl_scr = rest[levels + 4 + levels :]
    step = pl.program_id(0)
    rows = q_ref.shape[0]
    picks = rows // RATE

    @pl.when(step == 0)
    def _():
        sums = functools.reduce(jnp.add, [ref[...] for ref in gathered])
        inv_row = lax.rsqrt(sums[0:1, :] / width + EPS)
        inv_scr[...] = as_columns(inv_row)
        cc_scr[...] = as_columns(inv_row * inv_row * (sums[1:2, :] / width))

    subs = range(per)
    deltas = []
    for sub in subs:
        head = step * per + sub
        near_col, far_col = pair_columns(rate_ref[pl.ds(head, 1), :], rate_ref[pl.ds(head + heads, 1), :])
        gain = lanes(gain_ref, sub)[...]
        att = att_ref[sub]
        inv = inv_scr[...]
        lanes(normed_ref, sub)[...] = (att * inv * gain).astype(BF16)
        scaled = lanes(og_ref, sub)[...].astype(F32) * gain
        grad_att = inv * (scaled - att * cc_scr[...])
        ga_near = (grad_att * near_col).astype(BF16)
        ga_far = (grad_att * far_col).astype(BF16)
        ga_ref[sub] = ga_near
        gf_scr[sub] = ga_far
        delta_near = jnp.sum(ga_near.astype(F32) * att, axis=1, keepdims=True)
        delta_ref[sub] = jnp.broadcast_to(delta_near, (rows, LANES))
        deltas.append(jnp.sum((ga_far.astype(F32) * att).T, axis=0, keepdims=True))
    for sub in subs:
        for level in range(levels):
            span = slice(level * picks, (level + 1) * picks)
            grad_w = dot_nt(recv[level][sub, 1], gf_scr[sub])
            gl_scr[sub, span, :] = (ef_ref[sub, span, :].astype(F32) * (grad_w - deltas[sub])).astype(BF16)
    for sub in subs:
        keys = jnp.concatenate([ref[sub, 0] for ref in recv], axis=0)
        dq_ref[sub] = dot_tn(gl_scr[sub], keys)
        dk = dot_nn(gl_scr[sub], lanes(q_ref, sub)[...]) * SCALE
        dv = dot_nn(ef_ref[sub], gf_scr[sub])
        for level, out in enumerate(outs):
            out[sub, 0] = dk[level * picks : (level + 1) * picks].astype(BF16)
            out[sub, 1] = dv[level * picks : (level + 1) * picks].astype(BF16)


def fold(wide, far):
    return ((wide[:, :DH] + wide[:, DH:] + far) * SCALE).astype(BF16)


def backward_near_kernel(e_ref, ga_ref, delta_ref, q_ref, k_ref, v_ref, dqf_ref, dq_ref, dk_ref, dv_ref, gl_scr, k_scr):
    rows = q_ref.shape[0]

    @pl.when(pl.program_id(0) == 0)
    def _():
        k_scr[:, DH:] = jnp.zeros((rows, DH), BF16)

    k_scr[:, :DH] = k_ref[...]
    waiting = []
    for start in range(0, rows, TQ):
        part = pl.ds(start, TQ)
        grad_w = dot_nt(ga_ref[0, part, :], v_ref[...])
        for done in waiting:
            dq_ref[done, :] = fold(dot_nn(gl_scr[done, :], k_scr[...]), dqf_ref[0, done, :])
        delta = jnp.concatenate([delta_ref[0, part, :]] * (rows // LANES), axis=1)
        gl_scr[part, :] = (e_ref[0, part, :].astype(F32) * (grad_w - delta)).astype(BF16)
        waiting = [part]
    for done in waiting:
        dq_ref[done, :] = fold(dot_nn(gl_scr[done, :], k_scr[...]), dqf_ref[0, done, :])
    dk_ref[0] = dot_nn(q_ref[...].T, gl_scr[...]).T * SCALE
    dv_ref[0] = dot_nn(ga_ref[0].T, e_ref[0]).T


def merge_kernel(levels, per, off_ref, dk_ref, dv_ref, *rest):
    back = rest[:levels]
    gk_ref, gv_ref, k_scr, v_scr = rest[levels:]
    step = pl.program_id(0)
    picks = dk_ref.shape[1] // RATE
    for sub in range(per):
        k_scr[...] = dk_ref[sub]
        v_scr[...] = dv_ref[sub]
        for level in range(levels):
            spot = pl.ds(off_ref[level, step * per + sub], picks, stride=RATE)
            k_scr[spot, :] += back[level][sub, 0].astype(F32)
            v_scr[spot, :] += back[level][sub, 1].astype(F32)
        lanes(gk_ref, sub)[...] = k_scr[...].astype(BF16)
        lanes(gv_ref, sub)[...] = v_scr[...].astype(BF16)


def local(queries, key_rows, value_rows, out_grad, norm_gain, offsets, segments, tile_mask):
    rows = queries.shape[0]
    blocks = lax.axis_size("ctx")
    seg_rows = segments.reshape(-1, LANES)
    width = queries.shape[1]
    heads = width // DH
    picks = rows // RATE
    per = 4 if heads % 4 == 0 else 1
    smem = pl.BlockSpec(memory_space=pltpu.SMEM)
    wide = pl.BlockSpec((rows, per * DH), lambda h: (0, h))
    pair = pl.BlockSpec((per, 2, picks, DH), lambda h: (h, 0, 0, 0))
    pair_shape = jax.ShapeDtypeStruct((heads, 2, picks, DH), BF16)
    branch, *samples = pl.pallas_call(
        functools.partial(sample_kernel, per, blocks, rows),
        name="sample",
        grid=(heads // per,),
        in_specs=[smem, smem, wide, wide],
        out_specs=[smem] + [pair] * LEVELS,
        out_shape=[jax.ShapeDtypeStruct((1,), jnp.int32)] + [pair_shape] * LEVELS,
        scratch_shapes=[pltpu.VMEM((rows, DH), F32)] * 2,
        compiler_params=pltpu.CompilerParams(dimension_semantics=("arbitrary",), vmem_limit_bytes=12 << 20),
        cost_estimate=pl.CostEstimate(flops=0, bytes_accessed=6 * rows * width, transcendentals=0),
    )(pltpu.with_memory_space_constraint(segments, pltpu.HBM), offsets, *(pltpu.with_memory_space_constraint(x, pltpu.HBM) for x in (key_rows, value_rows)))
    own = lax.axis_index("ctx").reshape(1)
    args = (queries, key_rows, value_rows, out_grad, norm_gain, offsets, seg_rows, tile_mask, own, samples)
    return lax.switch(branch[0], [functools.partial(layer, count + 1) for count in range(LEVELS)], *args)


def layer(levels, queries, key_rows, value_rows, out_grad, norm_gain, offsets, seg_rows, tile_mask, own, samples):
    rows, width = queries.shape
    heads = width // DH
    picks = rows // RATE
    total_width = width * lax.axis_size("head")
    queries, key_rows, value_rows, out_grad = [
        pltpu.with_memory_space_constraint(x, pltpu.HBM) for x in (queries, key_rows, value_rows, out_grad)
    ]

    by_head = pl.BlockSpec((rows, DH), lambda h: (0, h))
    seg_spec = pl.BlockSpec(seg_rows.shape, lambda h: (0, 0))
    pair = pl.BlockSpec((1, 2, picks, DH), lambda h: (h, 0, 0, 0))
    major = pl.BlockSpec((1, rows, DH), lambda h: (h, 0, 0))
    major_f = jax.ShapeDtypeStruct((heads, rows, DH), F32)
    major_b = jax.ShapeDtypeStruct((heads, rows, DH), BF16)
    per = 2 if heads % 2 == 0 else 1
    wide_n = pl.BlockSpec((rows, per * DH), lambda h: (0, h))
    major_n = pl.BlockSpec((per, rows, DH), lambda h: (h, 0, 0))
    pair_n = pl.BlockSpec((per, 2, picks, DH), lambda h: (h, 0, 0, 0))
    stat_rows = pl.BlockSpec((2 * heads, rows), lambda h: (0, 0))
    smem = pl.BlockSpec(memory_space=pltpu.SMEM)
    gain_row = norm_gain.reshape(1, width)
    gain_spec = pl.BlockSpec((1, per * DH), lambda h: (0, h))

    def call(kernel, name, mib, in_specs, out_specs, out_shape, scratch=(), flops=0, moved=0, expo=0, per=1):
        return pl.pallas_call(
            kernel,
            name=name,
            grid=(heads // per,),
            in_specs=in_specs,
            out_specs=out_specs,
            out_shape=out_shape,
            scratch_shapes=scratch,
            compiler_params=pltpu.CompilerParams(dimension_semantics=("arbitrary",), vmem_limit_bytes=mib << 20),
            cost_estimate=pl.CostEstimate(flops=flops, bytes_accessed=moved, transcendentals=expo),
        )

    def shape(dims, dtype):
        return jax.ShapeDtypeStruct(dims, dtype)

    full = rows * width
    pair_shape = shape((heads, 2, picks, DH), BF16)
    recv = [partner(samples[level], "ctx", level) for level in range(levels)]

    square = rows * rows * heads
    expo, acc, stat = call(
        functools.partial(forward_near_kernel, heads),
        "forward_near",
        12,
        [smem, by_head, by_head, by_head, seg_spec],
        [pl.BlockSpec((1, rows, rows), lambda h: (h, 0, 0)), major, stat_rows],
        [pltpu.HBM((heads, rows, rows), BF16), major_f, shape((2 * heads, rows), F32)],
        [pltpu.VMEM((rows, 2 * DH), BF16)] * 3 + [pltpu.VMEM((rows, LANES), F32)],
        flops=4 * square * DH,
        moved=2 * square + 10 * full,
        expo=square,
    )(own, queries, key_rows, value_rows, seg_rows)

    far_n = levels * picks
    far_spec = pl.BlockSpec((per, far_n, rows), lambda h: (h, 0, 0))
    far_square = rows * far_n * heads
    att, expo_far, rate, sums = call(
        functools.partial(forward_far_kernel, heads, levels, per),
        "forward_far",
        18,
        [smem, smem, smem, wide_n, seg_spec, major_n, stat_rows, wide_n, gain_spec]
        + [pair_n] * levels,
        [major_n, far_spec, stat_rows, pl.BlockSpec((2, rows), lambda h: (0, 0))],
        [major_f, shape((heads, far_n, rows), BF16), shape((2 * heads, rows), F32), shape((2, rows), F32)],
        [pltpu.VMEM((levels, rows), F32)]
        + [pltpu.VMEM((rows, LANES), F32)] * levels,
        flops=4 * far_square * DH,
        moved=2 * far_square + 12 * full,
        per=per,
        expo=far_square,
    )(own, offsets, tile_mask, queries, seg_rows, acc, stat, out_grad, gain_row, *recv)
    parts = lax.axis_size("head")
    shifted = [
        lax.ppermute(sums, "head", [(i, (i + step) % parts) for i in range(parts)]) for step in range(1, parts)
    ]
    gathered = [sums] + shifted

    outs = call(
        functools.partial(backward_far_kernel, heads, levels, per, total_width, parts),
        "backward_far",
        18,
        [pl.BlockSpec((2, rows), lambda h: (0, 0))] * parts
        + [major_n, wide_n, gain_spec, stat_rows, wide_n, far_spec]
        + [pair_n] * levels,
        [wide_n, major_n, major_n, major_n] + [pair_n] * levels,
        [shape((rows, width), BF16), major_b, major_f, major_f]
        + [pair_shape] * levels,
        [pltpu.VMEM((rows, LANES), F32)] * 2
        + [pltpu.VMEM((per, rows, DH), BF16), pltpu.VMEM((per, far_n, rows), BF16)],
        flops=8 * far_square * DH,
        moved=2 * far_square + 16 * full,
        per=per,
    )(*gathered, att, out_grad, gain_row, rate, queries, expo_far, *recv)
    normed, grad_att, delta, dq_far = outs[:4]
    back = [partner(outs[4 + level], "ctx", level) for level in range(levels)]

    grad_queries, dk, dv = call(
        backward_near_kernel,
        "backward_near",
        20,
        [pl.BlockSpec((1, rows, rows), lambda h: (h, 0, 0)), major, major, by_head, by_head, by_head, major],
        [by_head, major, major],
        [shape((rows, width), BF16), major_f, major_f],
        [pltpu.VMEM((rows, rows), BF16), pltpu.VMEM((rows, 2 * DH), BF16)],
        flops=8 * square * DH,
        moved=2 * square + 22 * full,
    )(pltpu.with_memory_space_constraint(expo, pltpu.HBM), grad_att, delta, queries, key_rows, value_rows, dq_far)

    grad_keys, grad_values = call(
        functools.partial(merge_kernel, levels, per),
        "merge",
        11,
        [smem, major_n, major_n] + [pair_n] * levels,
        [wide_n, wide_n],
        [shape((rows, width), BF16)] * 2,
        [pltpu.VMEM((rows, DH), F32)] * 2,
        moved=14 * full,
        per=per,
    )(offsets, dk, dv, *back)
    return (normed, grad_queries, grad_keys, grad_values)


def solution(mesh):
    placed = (
        P("ctx", "head"),
        P("ctx", "head"),
        P("ctx", "head"),
        P("ctx", "head"),
        P("head"),
        P(None, "head"),
        P(),
        P("ctx", None),
    )
    return jax.shard_map(
        local,
        mesh=mesh,
        in_specs=placed,
        out_specs=(P("ctx", "head"), P("ctx", "head"), P("ctx", "head"), P("ctx", "head")),
        check_vma=False,
    )
```

```python
import functools

import jax
import jax.numpy as jnp
from jax import lax
from jax.experimental import pallas as pl
from jax.experimental.pallas import tpu as pltpu
from jax.sharding import PartitionSpec as P

DH = 128
RATE = 8
LEVELS = 3
LANES = 128
BIG = 1e30
EPS = 1e-06
TQ = 256
GROUP = 2
SUM_LIMIT = 2.0**60
F32 = jnp.float32
BF16 = jnp.bfloat16
SCALE = DH ** (-0.5)
EXP2_SCALE = SCALE * 1.4426950408889634


def partner(value, axis, bit):
    mask = 2**bit
    pairs = [(source, source ^ mask) for source in range(lax.axis_size(axis))]
    return lax.ppermute(value, axis, pairs)


def dot_nt(a, b):
    return lax.dot_general(a, b, (((1,), (1,)), ((), ())), preferred_element_type=F32)


def dot_nn(a, b):
    return lax.dot_general(a, b, (((1,), (0,)), ((), ())), preferred_element_type=F32)


def dot_tn(a, b):
    return lax.dot_general(a, b, (((0,), (0,)), ((), ())), preferred_element_type=F32)


def lane_of(shape):
    return lax.broadcasted_iota(jnp.int32, shape, 1)


def lanes(ref, sub):
    return ref.at[:, pl.ds(sub * DH, DH)]


def lead(ref, sub):
    return ref.at[pl.ds(sub, 1)]


def sample_kernel(per, blocks, rows, seg_ref, off_ref, k_ref, v_ref, branch_ref, *rest):
    outs, (k_scr, v_scr) = rest[:-2], rest[-2:]
    step = pl.program_id(0)
    picks = rows // RATE

    @pl.when(step == 0)
    def _():
        first = [seg_ref[block * rows] for block in range(blocks)]
        last = [seg_ref[block * rows + rows - 1] for block in range(blocks)]
        branch = jnp.int32(0)
        for level in range(1, LEVELS):
            meet = jnp.int32(0)
            for block in range(blocks):
                other = block ^ 2**level
                if block < other:
                    near = jnp.maximum(first[block], first[other]) <= jnp.minimum(last[block], last[other])
                    meet = jnp.where(near, jnp.int32(1), meet)
            branch = jnp.where(meet == 1, jnp.int32(level), branch)
        branch_ref[0] = branch

    for sub in range(per):
        k_scr[...] = lanes(k_ref, sub)[...].astype(F32)
        v_scr[...] = lanes(v_ref, sub)[...].astype(F32)
        for level, out in enumerate(outs):
            start = off_ref[level, step * per + sub]
            out[sub, 0] = k_scr[pl.ds(start, picks, stride=RATE), :].astype(BF16)
            out[sub, 1] = v_scr[pl.ds(start, picks, stride=RATE), :].astype(BF16)


def as_columns(row):
    return jnp.broadcast_to(row, (LANES, row.shape[1])).T


def forward_near_kernel(
    heads, own_ref, q_ref, k_ref, v_ref, seg_ref, e_ref, acc_ref, stat_ref, qa_scr, ka_scr, va_scr, stat_scr
):
    head = pl.program_id(0)
    rows = q_ref.shape[0]

    @pl.when(head == 0)
    def _():
        same = as_columns(segment_row(seg_ref, own_ref[0], rows)) == lane_of((rows, LANES)).astype(F32)
        qa_scr[:, DH:] = jnp.where(same, 1.0, 0.0).astype(BF16)
        ka_scr[:, DH:] = jnp.where(same, 0.0, -BIG).astype(BF16)
        va_scr[:, DH:] = jnp.ones((rows, LANES), BF16)

    qa_scr[:, :DH] = q_ref[...]
    ka_scr[:, :DH] = k_ref[...]
    va_scr[:, :DH] = v_ref[...]

    def weigh(parts, pick):
        every = [dot_nt(qa_scr[part, :], ka_scr[...]) for part in parts]
        return every, [pick(part, logits) for part, logits in zip(parts, every)]

    def expose(parts, every, shifts):
        for part, logits, shift in zip(parts, every, shifts):
            e_ref[0, part, :] = jnp.exp2((logits - shift) * EXP2_SCALE).astype(BF16)

    def mix(parts, shifts):
        lane = lane_of((TQ, LANES))
        sums = []
        for part, shift in zip(parts, shifts):
            mixed = dot_nn(e_ref[0, part, :], va_scr[...])
            acc_ref[0, part, :] = mixed[:, :DH]
            kept = jnp.where(lane == head + heads, mixed[:, DH:], stat_scr[part, :])
            stat_scr[part, :] = jnp.where(lane == head, shift, kept)
            sums.append(mixed[:, DH:])
        return sums

    def own_logit(part, logits):
        return jnp.sum(q_ref[part, :].astype(F32) * k_ref[part, :].astype(F32), axis=1, keepdims=True)

    def top_logit(part, logits):
        return jnp.max(logits, axis=1, keepdims=True)

    sums, waiting = [], None
    for start in range(0, rows, GROUP * TQ):
        parts = [pl.ds(start + index * TQ, TQ) for index in range(GROUP)]
        every, shifts = weigh(parts, own_logit)
        if waiting is not None:
            sums += mix(*waiting)
        expose(parts, every, shifts)
        waiting = (parts, shifts)
    sums += mix(*waiting)
    safe = jnp.max(functools.reduce(jnp.maximum, sums)) <= SUM_LIMIT

    @pl.when(jnp.logical_not(safe))
    def _():
        @pl.loop(0, rows // TQ)
        def _(index):
            parts = [pl.ds(pl.multiple_of(index * TQ, TQ), TQ)]
            every, shifts = weigh(parts, top_logit)
            expose(parts, every, shifts)
            mix(parts, shifts)

    @pl.when(head == pl.num_programs(0) - 1)
    def _():
        stat_ref[...] = stat_scr[...].T[: 2 * heads, :]


def segment_row(ref, block, rows):
    depth = rows // LANES
    part = ref[pl.ds(pl.multiple_of(block * depth, depth), depth), :].astype(F32)
    return jnp.concatenate([part[i : i + 1, :] for i in range(depth)], axis=1)


def split_parts(x, count):
    parts = []
    for _ in range(count):
        piece = x.astype(BF16)
        parts.append(piece)
        x = x - piece.astype(F32)
    return parts


def row_sums(x, count):
    ones = jnp.ones((16, x.shape[1]), BF16)
    return sum(dot_nt(ones, piece) for piece in split_parts(x, count))[0:1, :]


def pair_columns(first, second):
    pieces = split_parts(first, 3) + split_parts(second, 3)
    rows = jnp.concatenate(pieces + [jnp.zeros((10, first.shape[1]), BF16)], axis=0)
    source = lax.broadcasted_iota(jnp.int32, (16, 2 * LANES), 0)
    lane = lane_of((16, 2 * LANES))
    spread = jnp.where((source < 3) == (lane < LANES), 1.0, 0.0).astype(BF16)
    wide = dot_tn(rows, spread)
    return wide[:, :LANES], wide[:, LANES:]


def forward_far_kernel(
    heads, levels, per, own_ref, off_ref, mask_ref, q_ref, seg_ref, acc_ref, stat_ref, og_ref, gain_ref, *rest
):
    recv = rest[:levels]
    att_ref, ef_ref, rate_ref, sums_ref, open_scr = rest[levels : levels + 5]
    seg_scr = rest[levels + 5 :]
    step = pl.program_id(0)
    rows = q_ref.shape[0]
    picks = rows // RATE
    tiles = mask_ref.shape[0]
    tile = rows // tiles

    @pl.when(step == 0)
    def _():
        sums_ref[...] = jnp.zeros_like(sums_ref)
        own = own_ref[0]
        own_row = segment_row(seg_ref, own, rows)
        for level in range(levels):
            other = jnp.bitwise_xor(own, 2**level)
            seg_scr[level][...] = as_columns(segment_row(seg_ref, other, rows))
            for index in range(tiles):
                span = slice(index * tile, (index + 1) * tile)
                shut = jnp.where(mask_ref[index, level] == 1, 0.0, 1.0)
                open_scr[level : level + 1, span] = own_row[:, span] - 1000.0 * shut

    subs = range(per)
    scores, sums = [], []
    for sub in subs:
        found = []
        for level in range(levels):
            picked = seg_scr[level][pl.ds(off_ref[level, step * per + sub], picks, stride=RATE), :]
            same = jnp.concatenate([picked] * (rows // LANES), axis=1) == open_scr[level : level + 1, :]
            part = dot_nt(recv[level][sub, 0], lanes(q_ref, sub)[...])
            found.append(jnp.where(same, part, -BIG))
        scores.append(found)
    tops = [functools.reduce(jnp.maximum, [jnp.max(x, axis=0, keepdims=True) for x in found]) for found in scores]
    for sub in subs:
        for level in range(levels):
            expo = jnp.exp2((scores[sub][level] - tops[sub]) * EXP2_SCALE).astype(BF16)
            ef_ref[sub, level * picks : (level + 1) * picks, :] = expo
    mixes = []
    for sub in subs:
        values = jnp.concatenate([ref[sub, 1] for ref in recv], axis=0)
        mixes.append(dot_tn(ef_ref[sub], values))
        ones = jnp.ones((16, levels * picks), BF16)
        sums.append(dot_nn(ones, ef_ref[sub])[0:1, :])
    columns = []
    for sub in subs:
        head = step * per + sub
        top_near = stat_ref[pl.ds(head, 1), :]
        sum_near = stat_ref[pl.ds(head + heads, 1), :]
        top = jnp.maximum(top_near, tops[sub])
        a_near = jnp.exp2((top_near - top) * EXP2_SCALE)
        a_far = jnp.exp2((tops[sub] - top) * EXP2_SCALE)
        inv = 1.0 / (a_near * sum_near + a_far * sums[sub])
        r_near = a_near * inv
        r_far = a_far * inv
        rate_ref[pl.ds(head, 1), :] = r_near
        rate_ref[pl.ds(head + heads, 1), :] = r_far
        columns.append(pair_columns(r_near, r_far))
    squares, crosses = [], []
    for sub in subs:
        att = columns[sub][0] * acc_ref[sub] + columns[sub][1] * mixes[sub]
        att_ref[sub] = att
        scaled = lanes(og_ref, sub)[...].astype(F32) * lanes(gain_ref, sub)[...]
        squares.append(att * att)
        crosses.append(scaled * att)
    sums_ref[0:1, :] += row_sums(functools.reduce(jnp.add, squares), 2)
    sums_ref[1:2, :] += row_sums(functools.reduce(jnp.add, crosses), 2)


def backward_far_kernel(heads, levels, per, width, parts, *refs):
    gathered = refs[:parts]
    att_ref, og_ref, gain_ref, rate_ref, q_ref, ef_ref = refs[parts : parts + 6]
    rest = refs[parts + 6 :]
    recv = rest[:levels]
    normed_ref, ga_ref, delta_ref, dq_ref = rest[levels : levels + 4]
    outs = rest[levels + 4 : levels + 4 + levels]
    inv_scr, cc_scr, gf_scr, gl_scr = rest[levels + 4 + levels :]
    step = pl.program_id(0)
    rows = q_ref.shape[0]
    picks = rows // RATE

    @pl.when(step == 0)
    def _():
        sums = functools.reduce(jnp.add, [ref[...] for ref in gathered])
        inv_row = lax.rsqrt(sums[0:1, :] / width + EPS)
        inv_scr[...] = as_columns(inv_row)
        cc_scr[...] = as_columns(inv_row * inv_row * (sums[1:2, :] / width))

    subs = range(per)
    deltas = []
    for sub in subs:
        head = step * per + sub
        near_col, far_col = pair_columns(rate_ref[pl.ds(head, 1), :], rate_ref[pl.ds(head + heads, 1), :])
        gain = lanes(gain_ref, sub)[...]
        att = att_ref[sub]
        inv = inv_scr[...]
        lanes(normed_ref, sub)[...] = (att * inv * gain).astype(BF16)
        scaled = lanes(og_ref, sub)[...].astype(F32) * gain
        grad_att = inv * (scaled - att * cc_scr[...])
        ga_near = (grad_att * near_col).astype(BF16)
        ga_far = (grad_att * far_col).astype(BF16)
        ga_ref[sub] = ga_near
        gf_scr[sub] = ga_far
        delta_near = jnp.sum(ga_near.astype(F32) * att, axis=1, keepdims=True)
        delta_ref[sub] = jnp.broadcast_to(delta_near, (rows, LANES))
        deltas.append(jnp.sum((ga_far.astype(F32) * att).T, axis=0, keepdims=True))
    for sub in subs:
        for level in range(levels):
            span = slice(level * picks, (level + 1) * picks)
            grad_w = dot_nt(recv[level][sub, 1], gf_scr[sub])
            gl_scr[sub, span, :] = (ef_ref[sub, span, :].astype(F32) * (grad_w - deltas[sub])).astype(BF16)
    for sub in subs:
        keys = jnp.concatenate([ref[sub, 0] for ref in recv], axis=0)
        dq_ref[sub] = dot_tn(gl_scr[sub], keys)
        dk = dot_nn(gl_scr[sub], lanes(q_ref, sub)[...]) * SCALE
        dv = dot_nn(ef_ref[sub], gf_scr[sub])
        for level, out in enumerate(outs):
            out[sub, 0] = dk[level * picks : (level + 1) * picks].astype(BF16)
            out[sub, 1] = dv[level * picks : (level + 1) * picks].astype(BF16)


def backward_near_kernel(e_ref, ga_ref, delta_ref, q_ref, k_ref, v_ref, dqf_ref, dq_ref, dk_ref, dv_ref, gl_scr):
    rows = q_ref.shape[0]
    span = 2 * TQ
    query_t = q_ref[...].T
    grad_t = ga_ref[0].T
    for start in range(0, rows, span):
        part = pl.ds(start, span)
        grad_w = dot_nt(ga_ref[0, part, :], v_ref[...])
        delta = jnp.concatenate([delta_ref[0, part, :]] * (rows // LANES), axis=1)
        gl_scr[part, :] = (e_ref[0, part, :].astype(F32) * (grad_w - delta)).astype(BF16)
    dk_ref[0] = dot_nn(query_t, gl_scr[...]).T * SCALE
    dv_ref[0] = dot_nn(grad_t, e_ref[0]).T
    dq_ref[...] = ((dot_nn(gl_scr[...], k_ref[...]) + dqf_ref[0]) * SCALE).astype(BF16)


def merge_kernel(levels, per, off_ref, dk_ref, dv_ref, *rest):
    back = rest[:levels]
    gk_ref, gv_ref, k_scr, v_scr = rest[levels:]
    step = pl.program_id(0)
    picks = dk_ref.shape[1] // RATE
    for sub in range(per):
        k_scr[...] = dk_ref[sub]
        v_scr[...] = dv_ref[sub]
        for level in range(levels):
            spot = pl.ds(off_ref[level, step * per + sub], picks, stride=RATE)
            k_scr[spot, :] += back[level][sub, 0].astype(F32)
            v_scr[spot, :] += back[level][sub, 1].astype(F32)
        lanes(gk_ref, sub)[...] = k_scr[...].astype(BF16)
        lanes(gv_ref, sub)[...] = v_scr[...].astype(BF16)


def local(queries, key_rows, value_rows, out_grad, norm_gain, offsets, segments, tile_mask):
    rows = queries.shape[0]
    blocks = lax.axis_size("ctx")
    seg_rows = segments.reshape(-1, LANES)
    width = queries.shape[1]
    heads = width // DH
    picks = rows // RATE
    per = 4 if heads % 4 == 0 else 1
    smem = pl.BlockSpec(memory_space=pltpu.SMEM)
    wide = pl.BlockSpec((rows, per * DH), lambda h: (0, h))
    pair = pl.BlockSpec((per, 2, picks, DH), lambda h: (h, 0, 0, 0))
    pair_shape = jax.ShapeDtypeStruct((heads, 2, picks, DH), BF16)
    branch, *samples = pl.pallas_call(
        functools.partial(sample_kernel, per, blocks, rows),
        name="sample",
        grid=(heads // per,),
        in_specs=[smem, smem, wide, wide],
        out_specs=[smem] + [pair] * LEVELS,
        out_shape=[jax.ShapeDtypeStruct((1,), jnp.int32)] + [pair_shape] * LEVELS,
        scratch_shapes=[pltpu.VMEM((rows, DH), F32)] * 2,
        compiler_params=pltpu.CompilerParams(dimension_semantics=("arbitrary",), vmem_limit_bytes=12 << 20),
        cost_estimate=pl.CostEstimate(flops=0, bytes_accessed=6 * rows * width, transcendentals=0),
    )(pltpu.with_memory_space_constraint(segments, pltpu.HBM), offsets, *(pltpu.with_memory_space_constraint(x, pltpu.HBM) for x in (key_rows, value_rows)))
    own = lax.axis_index("ctx").reshape(1)
    args = (queries, key_rows, value_rows, out_grad, norm_gain, offsets, seg_rows, tile_mask, own, samples)
    return lax.switch(branch[0], [functools.partial(layer, count + 1) for count in range(LEVELS)], *args)


def layer(levels, queries, key_rows, value_rows, out_grad, norm_gain, offsets, seg_rows, tile_mask, own, samples):
    rows, width = queries.shape
    heads = width // DH
    picks = rows // RATE
    total_width = width * lax.axis_size("head")
    queries, key_rows, value_rows, out_grad = [
        pltpu.with_memory_space_constraint(x, pltpu.HBM) for x in (queries, key_rows, value_rows, out_grad)
    ]

    by_head = pl.BlockSpec((rows, DH), lambda h: (0, h))
    seg_spec = pl.BlockSpec(seg_rows.shape, lambda h: (0, 0))
    pair = pl.BlockSpec((1, 2, picks, DH), lambda h: (h, 0, 0, 0))
    major = pl.BlockSpec((1, rows, DH), lambda h: (h, 0, 0))
    major_f = jax.ShapeDtypeStruct((heads, rows, DH), F32)
    major_b = jax.ShapeDtypeStruct((heads, rows, DH), BF16)
    per = 2 if heads % 2 == 0 else 1
    wide_n = pl.BlockSpec((rows, per * DH), lambda h: (0, h))
    major_n = pl.BlockSpec((per, rows, DH), lambda h: (h, 0, 0))
    pair_n = pl.BlockSpec((per, 2, picks, DH), lambda h: (h, 0, 0, 0))
    stat_rows = pl.BlockSpec((2 * heads, rows), lambda h: (0, 0))
    smem = pl.BlockSpec(memory_space=pltpu.SMEM)
    gain_row = norm_gain.reshape(1, width)
    gain_spec = pl.BlockSpec((1, per * DH), lambda h: (0, h))

    def call(kernel, name, mib, in_specs, out_specs, out_shape, scratch=(), flops=0, moved=0, expo=0, per=1):
        return pl.pallas_call(
            kernel,
            name=name,
            grid=(heads // per,),
            in_specs=in_specs,
            out_specs=out_specs,
            out_shape=out_shape,
            scratch_shapes=scratch,
            compiler_params=pltpu.CompilerParams(dimension_semantics=("arbitrary",), vmem_limit_bytes=mib << 20),
            cost_estimate=pl.CostEstimate(flops=flops, bytes_accessed=moved, transcendentals=expo),
        )

    def shape(dims, dtype):
        return jax.ShapeDtypeStruct(dims, dtype)

    full = rows * width
    pair_shape = shape((heads, 2, picks, DH), BF16)
    recv = [partner(samples[level], "ctx", level) for level in range(levels)]

    square = rows * rows * heads
    expo, acc, stat = call(
        functools.partial(forward_near_kernel, heads),
        "forward_near",
        12,
        [smem, by_head, by_head, by_head, seg_spec],
        [pl.BlockSpec((1, rows, rows), lambda h: (h, 0, 0)), major, stat_rows],
        [pltpu.HBM((heads, rows, rows), BF16), major_f, shape((2 * heads, rows), F32)],
        [pltpu.VMEM((rows, 2 * DH), BF16)] * 3 + [pltpu.VMEM((rows, LANES), F32)],
        flops=4 * square * DH,
        moved=2 * square + 10 * full,
        expo=square,
    )(own, queries, key_rows, value_rows, seg_rows)

    far_n = levels * picks
    far_spec = pl.BlockSpec((per, far_n, rows), lambda h: (h, 0, 0))
    far_square = rows * far_n * heads
    att, expo_far, rate, sums = call(
        functools.partial(forward_far_kernel, heads, levels, per),
        "forward_far",
        18,
        [smem, smem, smem, wide_n, seg_spec, major_n, stat_rows, wide_n, gain_spec]
        + [pair_n] * levels,
        [major_n, far_spec, stat_rows, pl.BlockSpec((2, rows), lambda h: (0, 0))],
        [major_f, shape((heads, far_n, rows), BF16), shape((2 * heads, rows), F32), shape((2, rows), F32)],
        [pltpu.VMEM((levels, rows), F32)]
        + [pltpu.VMEM((rows, LANES), F32)] * levels,
        flops=4 * far_square * DH,
        moved=2 * far_square + 12 * full,
        per=per,
        expo=far_square,
    )(own, offsets, tile_mask, queries, seg_rows, acc, stat, out_grad, gain_row, *recv)
    parts = lax.axis_size("head")
    shifted = [
        lax.ppermute(sums, "head", [(i, (i + step) % parts) for i in range(parts)]) for step in range(1, parts)
    ]
    gathered = [sums] + shifted

    outs = call(
        functools.partial(backward_far_kernel, heads, levels, per, total_width, parts),
        "backward_far",
        18,
        [pl.BlockSpec((2, rows), lambda h: (0, 0))] * parts
        + [major_n, wide_n, gain_spec, stat_rows, wide_n, far_spec]
        + [pair_n] * levels,
        [wide_n, major_n, major_n, major_n] + [pair_n] * levels,
        [shape((rows, width), BF16), major_b, major_f, major_f]
        + [pair_shape] * levels,
        [pltpu.VMEM((rows, LANES), F32)] * 2
        + [pltpu.VMEM((per, rows, DH), BF16), pltpu.VMEM((per, far_n, rows), BF16)],
        flops=8 * far_square * DH,
        moved=2 * far_square + 16 * full,
        per=per,
    )(*gathered, att, out_grad, gain_row, rate, queries, expo_far, *recv)
    normed, grad_att, delta, dq_far = outs[:4]
    back = [partner(outs[4 + level], "ctx", level) for level in range(levels)]

    grad_queries, dk, dv = call(
        backward_near_kernel,
        "backward_near",
        20,
        [pl.BlockSpec((1, rows, rows), lambda h: (h, 0, 0)), major, major, by_head, by_head, by_head, major],
        [by_head, major, major],
        [shape((rows, width), BF16), major_f, major_f],
        [pltpu.VMEM((rows, rows), BF16)],
        flops=8 * square * DH,
        moved=2 * square + 22 * full,
    )(pltpu.with_memory_space_constraint(expo, pltpu.HBM), grad_att, delta, queries, key_rows, value_rows, dq_far)

    grad_keys, grad_values = call(
        functools.partial(merge_kernel, levels, per),
        "merge",
        11,
        [smem, major_n, major_n] + [pair_n] * levels,
        [wide_n, wide_n],
        [shape((rows, width), BF16)] * 2,
        [pltpu.VMEM((rows, DH), F32)] * 2,
        moved=14 * full,
        per=per,
    )(offsets, dk, dv, *back)
    return (normed, grad_queries, grad_keys, grad_values)


def solution(mesh):
    placed = (
        P("ctx", "head"),
        P("ctx", "head"),
        P("ctx", "head"),
        P("ctx", "head"),
        P("head"),
        P(None, "head"),
        P(),
        P("ctx", None),
    )
    return jax.shard_map(
        local,
        mesh=mesh,
        in_specs=placed,
        out_specs=(P("ctx", "head"), P("ctx", "head"), P("ctx", "head"), P("ctx", "head")),
        check_vma=False,
    )
```
